32 devices in a mesh: groups: 2 (over y), ctx: 16 (over z, x, core).
Axes of the slice: x: 2, y: 2, z: 4, core: 2. Of those that a mesh axis runs over, the one named last changes fastest.
Arguments:
- queries: bfloat16 [8192, 4096], P(('groups', 'ctx')), parts along dimension 0, may hold values from -13 to 13
- all_key_states: bfloat16 [8192, 512], P(('groups', 'ctx')), parts along dimension 0, may hold values from -9.5 to 9.5
- all_value_states: bfloat16 [8192, 512], P(('groups', 'ctx')), parts along dimension 0, may hold values from -6 to 6
- selected: int32 [32, 2], P(('groups', 'ctx')), parts along dimension 0, may hold values from 0 to 14, as said below
Outputs:
- attended: bfloat16 [8192, 4096], P(('groups', 'ctx')), parts along dimension 0
The draws below stay inside these ranges and needn't reach their ends.
There are 2 independent parts, one for each index of `groups`. The reference program is written for one: setup_inputs(seed, part) draws one part's arguments, and reference() takes and returns one part's arrays. A program takes and returns all parts, laid end to end along the dimension named above; each array names one. Nothing has to cross between parts.
Inputs may be any that keep to these rules, and one draw needn't show every extreme that they name: `selected`: for block i >= 2 the two entries of row i are different blocks below i; rows 0 and 1 hold 0 and 0; the last block's first entry is 14.
All inputs are finite; a program needn't handle non-finite values.
Results may differ from the reference program's by a relative error of at most 0.004.
Values may be sent and summed in bfloat16 or wider, within the bound.
A program may use at most 64 MiB of HBM per device.

```python
import math
import jax
import jax.numpy as jnp
from jax import lax

QUERY_HEADS = 32
KEY_VALUE_HEADS = 4
HEAD_SIZE = 128
BLOCK_TOKENS = 256
NBLK = 16
CONTEXT_TOKENS = 4096


def draw_queries(key, part):
    random_component = jnp.clip(jax.random.normal(jax.random.fold_in(key, 1), (CONTEXT_TOKENS, QUERY_HEADS, HEAD_SIZE), jnp.float32), -4.0, 4.0) * 1.5
    return random_component.reshape(CONTEXT_TOKENS, QUERY_HEADS * HEAD_SIZE).astype(jnp.bfloat16)


def draw_all_key_states(key, part):
    random_component = jnp.clip(jax.random.normal(jax.random.fold_in(key, 4), (CONTEXT_TOKENS, KEY_VALUE_HEADS, HEAD_SIZE), jnp.float32), -6.0, 6.0)
    return random_component.reshape(CONTEXT_TOKENS, KEY_VALUE_HEADS * HEAD_SIZE).astype(jnp.bfloat16)


def draw_selected(key, part):
    block_position = jnp.arange(NBLK, dtype=jnp.int32)
    first_pick = jax.random.randint(jax.random.fold_in(key, 11), (NBLK,), 0, jnp.maximum(block_position, 1))
    first_pick = jnp.where(block_position == NBLK - 1, block_position - 1, first_pick)
    second_pick = jax.random.randint(jax.random.fold_in(key, 12), (NBLK,), 0, jnp.maximum(block_position - 1, 1))
    second_pick = second_pick + (second_pick >= first_pick).astype(jnp.int32)
    second_pick = jnp.where(block_position >= 2, second_pick, 0)
    return jnp.stack([first_pick, second_pick], axis=1).astype(jnp.int32)


def shard_levels(key, extent, split, low, high):
    def one(dim, shards_of):
        draws = jax.random.uniform(jax.random.fold_in(jax.random.fold_in(key, 6), dim), (shards_of,), jnp.float32, low / len(split), high / len(split))
        return jnp.repeat(jnp.exp(draws), extent[dim] // shards_of).reshape((-1,) + (1,) * (len(extent) - dim - 1))

    factor_of = one(*split[0])
    for cut in split[1:]:
        factor_of = factor_of * one(*cut)
    return factor_of


def scatter_about(key, dims, width, bound, shards=(), kind=jnp.bfloat16):
    drawn = jax.random.normal(key, dims, jnp.float32) * width
    if len(shards) > 0:
        drawn = shard_levels(key, dims, shards, -0.22, 0.18) * drawn
    return jnp.clip(drawn, min=-bound, max=bound).astype(kind)


def setup_inputs(seed: int = 0, part: int = 0) -> dict:
    keys = jax.random.split(jax.random.key(seed), 5)
    part_splits = jax.random.split(jax.random.fold_in(keys[4], part), 5)
    queries = draw_queries(jax.random.fold_in(jax.random.fold_in(keys[4], part), 71), part)
    all_key_states = draw_all_key_states(jax.random.fold_in(jax.random.fold_in(keys[4], part), 71), part)
    all_value_states = scatter_about(part_splits[2], (CONTEXT_TOKENS, KEY_VALUE_HEADS * HEAD_SIZE), 1.0, 6.0, ((0, 16),))
    selected = draw_selected(jax.random.fold_in(jax.random.fold_in(keys[4], part), 71), part)
    return dict(queries=queries, all_key_states=all_key_states, all_value_states=all_value_states, selected=selected)


def reference(queries, all_key_states, all_value_states, selected):
    group_width = QUERY_HEADS // KEY_VALUE_HEADS
    score_scale = 1.0 / math.sqrt(HEAD_SIZE)
    row_ids = jnp.arange(BLOCK_TOKENS, dtype=jnp.int32)
    causal = row_ids[None, :] <= row_ids[:, None]

    def rows_for_block(source, block_number):
        return lax.dynamic_slice_in_dim(source, (block_number * BLOCK_TOKENS).astype(jnp.int32), BLOCK_TOKENS, 0)

    def one_block(block_position):
        first_block = selected[block_position, 0]
        second_block = selected[block_position, 1]
        first_valid = first_block < block_position
        second_valid = jnp.logical_and(second_block < block_position, second_block != first_block)
        query_row_block = rows_for_block(queries, block_position).astype(jnp.float32).reshape(BLOCK_TOKENS, KEY_VALUE_HEADS, group_width, HEAD_SIZE)
        key_row_block = jnp.concatenate([rows_for_block(all_key_states, block_position), rows_for_block(all_key_states, first_block), rows_for_block(all_key_states, second_block)], axis=0)
        value_row_block = jnp.concatenate([rows_for_block(all_value_states, block_position), rows_for_block(all_value_states, first_block), rows_for_block(all_value_states, second_block)], axis=0)
        key_row_block = key_row_block.astype(jnp.float32).reshape(3 * BLOCK_TOKENS, KEY_VALUE_HEADS, HEAD_SIZE)
        value_row_block = value_row_block.astype(jnp.float32).reshape(3 * BLOCK_TOKENS, KEY_VALUE_HEADS, HEAD_SIZE)
        allowed = jnp.concatenate([causal, jnp.broadcast_to(first_valid, (BLOCK_TOKENS, BLOCK_TOKENS)), jnp.broadcast_to(second_valid, (BLOCK_TOKENS, BLOCK_TOKENS))], axis=1)
        scores = jnp.einsum('tgrd,ugd->tgru', query_row_block, key_row_block) * score_scale
        scores = jnp.where(allowed[:, None, None, :], scores, jnp.float32(-1e+30))
        row_max = lax.optimization_barrier(jnp.max(scores, axis=3, keepdims=True))
        weights = jnp.exp(scores - row_max)
        row_sum = lax.optimization_barrier(jnp.sum(weights, axis=3, keepdims=True))
        rounded = lax.optimization_barrier(weights.astype(jnp.bfloat16)).astype(jnp.float32)
        mixture = jnp.einsum('tgru,ugd->tgrd', rounded, value_row_block)
        return (mixture / row_sum).astype(jnp.bfloat16).reshape(BLOCK_TOKENS, QUERY_HEADS * HEAD_SIZE)
    result = lax.map(one_block, jnp.arange(NBLK, dtype=jnp.int32))
    return result.reshape(CONTEXT_TOKENS, QUERY_HEADS * HEAD_SIZE)
```

```python
import functools
import math

import jax
import jax.numpy as jnp
from jax import lax
from jax.experimental import pallas as pl
from jax.experimental.pallas import tpu as pltpu
from jax.sharding import PartitionSpec as P

QUERY_HEADS = 32
KEY_VALUE_HEADS = 4
HEAD_SIZE = 128
GROUP_WIDTH = QUERY_HEADS // KEY_VALUE_HEADS
EXPONENT_SCALE = math.log2(math.e) / math.sqrt(HEAD_SIZE)
MASKED = -1e30
LAYERS = 4
SIDE = 4
DIRECT = 3
MESH = pl.DeviceIdType.MESH


def half_max(scores):
    return jnp.maximum(scores[:, :HEAD_SIZE], scores[:, HEAD_SIZE:])


def weigh(queries, keys, causal, first_valid, second_valid):
    rows = queries.shape[0]
    scores = lax.dot_general(
        queries, keys, (((1,), (1,)), ((), ())), preferred_element_type=jnp.float32
    )
    own = jnp.where(causal, scores[:, :rows], MASKED)
    first = scores[:, rows : 2 * rows]
    second = scores[:, 2 * rows :]
    row_max = jnp.max(
        jnp.maximum(
            half_max(own),
            jnp.maximum(
                jnp.where(first_valid, half_max(first), MASKED),
                jnp.where(second_valid, half_max(second), MASKED),
            ),
        ),
        axis=1,
        keepdims=True,
    )
    first_max = jnp.where(first_valid, row_max, -MASKED)
    second_max = jnp.where(second_valid, row_max, -MASKED)
    return jnp.concatenate(
        [
            jnp.exp2((part - top) * EXPONENT_SCALE).astype(jnp.bfloat16)
            for part, top in ((own, row_max), (first, first_max), (second, second_max))
        ],
        axis=1,
    )


def mix(weights, values):
    mixture = jnp.dot(weights, values, preferred_element_type=jnp.float32)
    return (mixture[:, :HEAD_SIZE] * (1.0 / mixture[:, HEAD_SIZE:])).astype(jnp.bfloat16)


def attend_head(queries, keys, values, causal, first_valid, second_valid):
    return mix(weigh(queries, keys, causal, first_valid, second_valid), values)


def with_ones(values):
    return jnp.concatenate([values, jnp.ones_like(values)], axis=1)


def causal_mask(rows):
    return lax.broadcasted_iota(jnp.int32, (rows, rows), 1) <= lax.broadcasted_iota(
        jnp.int32, (rows, rows), 0
    )


def relay_kernel(rows, selected_hbm, query_hbm, key_hbm, value_hbm, out_ref, *scratch):
    heads = KEY_VALUE_HEADS
    chunks = 2 * heads
    stores = scratch[:chunks]
    outgoing = scratch[chunks : 2 * chunks]
    gathered = scratch[2 * chunks : 3 * chunks]
    (
        query_ref,
        weight_ref,
        request_vmem,
        request_smem,
        selected_ref,
        selected_sem,
        query_sem,
        pack_sem,
        local_sem,
        request_send,
        request_recv,
        spread_send,
        spread_recv,
        direct_send,
        direct_recv,
        chain_send,
        chain_recv,
        deliver_send,
        deliver_recv,
        dense_send,
        dense_recv,
    ) = scratch[3 * chunks :]
    quarter = rows // SIDE
    top = LAYERS - 1
    me = lax.axis_index("ctx")
    layer = me // SIDE
    place = me % SIDE
    mine = pl.ds(place * quarter, quarter)

    def on_layer(*layers):
        wanted = layer == layers[0]
        for other in layers[1:]:
            wanted = jnp.logical_or(wanted, layer == other)
        return pl.when(wanted)

    def peer(offset):
        return layer * SIDE + (place + offset) % SIDE

    def remote(src, dst, send, recv, target):
        return pltpu.make_async_remote_copy(
            src_ref=src,
            dst_ref=dst,
            send_sem=send,
            recv_sem=recv,
            device_id={"ctx": target},
            device_id_type=MESH,
        )

    def pack(c):
        source = (key_hbm, value_hbm)[c % 2]
        return pltpu.make_async_copy(
            source.at[:, pl.ds(c // 2 * HEAD_SIZE, HEAD_SIZE)],
            gathered[c].at[0],
            pack_sem.at[c],
        )

    def fetch_queries(g):
        columns = pl.ds(g * GROUP_WIDTH * HEAD_SIZE, GROUP_WIDTH * HEAD_SIZE)
        return pltpu.make_async_copy(
            query_hbm.at[:, columns], query_ref.at[:, columns], query_sem.at[g]
        )

    def request(offset):
        slot = request_vmem.at[place]
        return remote(
            slot, slot, request_send.at[offset - 1], request_recv.at[offset - 1], peer(offset)
        )

    def request_down(q):
        return remote(
            request_vmem.at[place],
            request_vmem.at[SIDE + place],
            request_send.at[SIDE - 1 + q],
            request_recv.at[SIDE - 1 + place],
            (top - 1) * SIDE + q,
        )

    def await_request(q):
        slot = request_vmem.at[SIDE + q]
        return remote(slot, slot, request_send.at[0], request_recv.at[SIDE - 1 + q], peer(1))

    def spread(c, offset):
        target = (place + offset) % SIDE
        return remote(
            gathered[c].at[0, pl.ds(target * quarter, quarter), :],
            stores[c].at[me],
            spread_send.at[c, offset - 1],
            spread_recv.at[c, offset - 1],
            peer(offset),
        )

    def direct(c, q):
        return remote(
            gathered[c].at[0, pl.ds(q * quarter, quarter), :],
            stores[c].at[me],
            direct_send.at[c, q],
            direct_recv.at[c, place],
            (layer + 1) % LAYERS * SIDE + q,
        )

    def await_direct(c, q):
        slot = stores[c].at[(layer + LAYERS - 1) % LAYERS * SIDE + q]
        return remote(slot, slot, direct_send.at[c, q], direct_recv.at[c, q], peer(1))

    def chain(c, source_layer, slot):
        part = stores[c].at[pl.ds(source_layer * SIDE, SIDE)]
        return remote(
            part,
            part,
            chain_send.at[c, slot],
            chain_recv.at[c, slot],
            (layer + 1) % LAYERS * SIDE + place,
        )

    def deliver(c, offset):
        return remote(
            outgoing[c].at[offset - 1],
            gathered[c].at[pl.ds(1, 2), mine, :],
            deliver_send.at[c, offset - 1],
            deliver_recv.at[c, offset - 1],
            peer(offset),
        )

    def choices_of(q):
        return (1,) if q == SIDE - 1 else (0, 1)

    def deliver_up(c, q, sender):
        span = len(choices_of(q))
        return remote(
            outgoing[c].at[SIDE - 1 + q, pl.ds(2 - span, span)],
            gathered[c].at[pl.ds(3 - span, span), pl.ds(sender * quarter, quarter), :],
            deliver_send.at[c, SIDE - 1 + q],
            deliver_recv.at[c, sender],
            top * SIDE + q,
        )

    def dense(c, source, target, slot, index):
        return remote(
            gathered[c].at[source],
            gathered[c].at[3 + slot],
            dense_send.at[c, index],
            dense_recv.at[c, slot],
            top * SIDE + target,
        )

    def dense_of(c, q):
        plan = {0: ((1, 0), (2, 0)), 1: ((3, 1),), 2: ((3, 2),), 3: ()}[q]
        return [dense(c, 0, target, slot, k) for k, (target, slot) in enumerate(plan)]

    def relay_of(c, q):
        return dense(c, 3, 3, 0, 1) if q == 2 else dense(c, 4, 2, 1, 0)

    def dense_in(c, slot):
        return dense(c, 3 + slot, 0, slot, 0)

    def on_place(q):
        return pl.when(me == top * SIDE + q)

    fetch_selected = pltpu.make_async_copy(selected_hbm, selected_ref, selected_sem)
    fetch_selected.start()
    for c in range(chunks):
        pack(c).start()
    for g in range(heads):
        fetch_queries(g).start()

    barrier = pltpu.get_barrier_semaphore()
    for offset in range(1, SIDE):
        pl.semaphore_signal(barrier, inc=1, device_id={"ctx": peer(offset)}, device_id_type=MESH)

    @pl.when(layer > 0)
    def _():
        for q in range(SIDE):
            pl.semaphore_signal(
                barrier, inc=1, device_id={"ctx": (layer - 1) * SIDE + q}, device_id_type=MESH
            )

    @pl.when(layer < top)
    def _():
        for q in range(SIDE):
            pl.semaphore_signal(
                barrier, inc=1, device_id={"ctx": (layer + 1) * SIDE + q}, device_id_type=MESH
            )

    neighbour_layers = jnp.minimum(layer, 1) + jnp.minimum(top - layer, 1)
    pl.semaphore_wait(barrier, SIDE - 1 + SIDE * neighbour_layers)

    fetch_selected.wait()
    lane = lax.broadcasted_iota(jnp.int32, (1, 128), 1)
    request_vmem[place] = jnp.where(lane == 0, selected_ref[0, 0], selected_ref[0, 1])

    @on_layer(top)
    def _():
        for q in range(SIDE):
            request_down(q).start()

    @pl.when(layer < top)
    def _():
        for offset in range(1, SIDE):
            request(offset).start()

    for c in range(chunks):
        pack(c).wait()

        if c < DIRECT:

            @on_layer(0, 1)
            def _():
                for q in range(SIDE):
                    direct(c, q).start()

        @pl.when(layer < top)
        def _():
            for offset in range(1, SIDE):
                spread(c, offset).start()
            stores[c][me] = gathered[c][0, mine, :]

        for q in range(SIDE - 1):

            @on_place(q)
            def _():
                for copy in dense_of(c, q):
                    copy.start()

    first_valid = selected_ref[0, 0] < me
    second_valid = jnp.logical_and(
        selected_ref[0, 1] < me, selected_ref[0, 1] != selected_ref[0, 0]
    )
    causal = causal_mask(rows)

    def slot_of(choice):
        wanted = selected_ref[0, choice]
        local = jnp.logical_and(layer == top, wanted >= top * SIDE)
        return jnp.where(local, 3 + wanted - top * SIDE, 1 + choice)

    def three(c):
        return jnp.concatenate(
            [gathered[c][0], gathered[c][slot_of(0)], gathered[c][slot_of(1)]], axis=0
        )

    def wait_spread(c):
        for offset in range(1, SIDE):
            spread(c, offset).wait_recv()

    def wait_below(c):
        if c < DIRECT:
            for q in range(SIDE):
                await_direct(c, q).wait_recv()
        else:
            chain(c, 0, 0).wait_recv()

    @pl.when(layer < top)
    def _():
        for offset in range(1, SIDE):
            request(offset).wait_recv()

    @on_layer(top - 1)
    def _():
        for q in range(SIDE):
            await_request(q).wait_recv()

    @pl.when(layer != top - 1)
    def _():
        for q in range(SIDE):
            request_vmem[SIDE + q] = jnp.zeros((1, 128), jnp.int32)

    @on_layer(top)
    def _():
        for offset in range(1, SIDE):
            request_vmem[(place + offset) % SIDE] = jnp.zeros((1, 128), jnp.int32)

    to_smem = pltpu.make_async_copy(request_vmem, request_smem, local_sem)
    to_smem.start()
    to_smem.wait()

    def hand_out(c):
        for offset in range(1, SIDE):
            for choice in range(2):
                wanted = request_smem[(place + offset) % SIDE, 0, choice]
                outgoing[c][offset - 1, choice] = stores[c][wanted]
            deliver(c, offset).start()
        for choice in range(2):
            gathered[c][1 + choice, mine, :] = stores[c][request_smem[place, 0, choice]]

    def hand_up(c):
        for q in range(SIDE):
            for choice in choices_of(q):
                wanted = jnp.minimum(request_smem[SIDE + q, 0, choice], top * SIDE - 1)
                outgoing[c][SIDE - 1 + q, choice] = stores[c][wanted]
            deliver_up(c, q, place).start()

    def serve_bottom(c):
        wait_spread(c)
        if c >= DIRECT:
            chain(c, 0, 0).start()
        hand_out(c)

    def serve_second(c):
        wait_below(c)
        chain(c, 0, 1).start()
        if c == 0:
            for early in range(DIRECT):
                wait_spread(early)
        if DIRECT <= c + 1 < chunks:
            wait_spread(c + 1)
            chain(c + 1, 1, 0).start()
        hand_out(c)

    def serve_third(c):
        wait_spread(c)
        if c < DIRECT:
            for q in range(SIDE):
                await_direct(c, q).wait_recv()
        else:
            chain(c, 1, 0).wait_recv()
        chain(c, 0, 1).wait_recv()
        hand_up(c)
        hand_out(c)

    def serve_top(c):
        for q in (2, 3):

            @on_place(q)
            def _():
                dense_in(c, q - 2).wait_recv()
                relay_of(c, q).start()

    def serve(step):
        for number, (work, ahead) in enumerate(
            ((serve_bottom, chunks), (serve_second, 3), (serve_third, 0), (serve_top, 3))
        ):
            begin = 0 if step == 0 else min(step + ahead, chunks)
            end = min(step + ahead + 1, chunks)
            if begin < end:

                @on_layer(number)
                def _():
                    for c in range(begin, end):
                        work(c)

    def wait_delivery(c):
        @pl.when(layer < top)
        def _():
            for offset in range(1, SIDE):
                deliver(c, offset).wait_recv()

        for q in range(SIDE):

            @on_place(q)
            def _():
                for sender in range(SIDE):
                    deliver_up(c, q, sender).wait_recv()
                for slot in {0: (), 1: (0,), 2: (1,), 3: (0, 2)}[q]:
                    if (q, slot) != (3, 1):
                        dense_in(c, slot).wait_recv()

    def compute(c):
        wait_delivery(c)
        g = c // 2
        if c % 2 == 0:
            fetch_queries(g).wait()
            keys = three(c)
            for index in range(GROUP_WIDTH):
                columns = pl.ds((g * GROUP_WIDTH + index) * HEAD_SIZE, HEAD_SIZE)
                weight_ref[index] = weigh(
                    query_ref[:, columns], keys, causal, first_valid, second_valid
                )
        else:
            values = with_ones(three(c))
            for index in range(GROUP_WIDTH):
                columns = pl.ds((g * GROUP_WIDTH + index) * HEAD_SIZE, HEAD_SIZE)
                out_ref[:, columns] = mix(weight_ref[index], values)

    for step in range(chunks):
        serve(step)
        if step > 0:
            compute(step - 1)
    compute(chunks - 1)

    @pl.when(layer < top)
    def _():
        for offset in range(1, SIDE):
            request(offset).wait_send()
        for c in range(chunks):
            for offset in range(1, SIDE):
                spread(c, offset).wait_send()
                deliver(c, offset).wait_send()

    @on_layer(0, 1)
    def _():
        for c in range(DIRECT):
            for q in range(SIDE):
                direct(c, q).wait_send()

    @on_layer(0)
    def _():
        for c in range(DIRECT, chunks):
            chain(c, 0, 0).wait_send()

    @on_layer(1)
    def _():
        for c in range(chunks):
            if c >= DIRECT:
                chain(c, 1, 0).wait_send()
            chain(c, 0, 1).wait_send()

    @on_layer(top - 1)
    def _():
        for c in range(chunks):
            for q in range(SIDE):
                deliver_up(c, q, place).wait_send()

    @on_layer(top)
    def _():
        for q in range(SIDE):
            request_down(q).wait_send()

    for q in range(SIDE):

        @on_place(q)
        def _():
            for c in range(chunks):
                for copy in dense_of(c, q):
                    copy.wait_send()
                if q >= 2:
                    relay_of(c, q).wait_send()


def relayed(queries, all_key_states, all_value_states, selected):
    rows = queries.shape[0]
    quarter = rows // SIDE
    chunks = 2 * KEY_VALUE_HEADS
    blocks = LAYERS * SIDE
    kind = all_key_states.dtype
    dma = pltpu.SemaphoreType.DMA
    return pl.pallas_call(
        functools.partial(relay_kernel, rows),
        out_shape=pltpu.VMEM(queries.shape, queries.dtype),
        in_specs=[pl.BlockSpec(memory_space=pltpu.HBM)] * 4,
        out_specs=pl.BlockSpec(memory_space=pltpu.VMEM),
        scratch_shapes=[pltpu.VMEM((blocks, quarter, HEAD_SIZE), kind)] * chunks
        + [pltpu.VMEM((2 * SIDE - 1, 2, quarter, HEAD_SIZE), kind)] * chunks
        + [pltpu.VMEM((6, rows, HEAD_SIZE), kind)] * chunks
        + [
            pltpu.VMEM(queries.shape, queries.dtype),
            pltpu.VMEM((GROUP_WIDTH, rows, 3 * rows), kind),
            pltpu.VMEM((2 * SIDE, 1, 128), jnp.int32),
            pltpu.SMEM((2 * SIDE, 1, 128), jnp.int32),
            pltpu.SMEM((1, 2), jnp.int32),
            dma,
            dma((KEY_VALUE_HEADS,)),
            dma((chunks,)),
            dma,
            dma((2 * SIDE - 1,)),
            dma((2 * SIDE - 1,)),
            dma((chunks, SIDE - 1)),
            dma((chunks, SIDE - 1)),
            dma((DIRECT, SIDE)),
            dma((DIRECT, SIDE)),
            dma((chunks, 2)),
            dma((chunks, 2)),
            dma((chunks, 2 * SIDE - 1)),
            dma((chunks, SIDE)),
            dma((chunks, 2)),
            dma((chunks, 3)),
        ],
        compiler_params=pltpu.CompilerParams(
            collective_id=0, has_side_effects=True, vmem_limit_bytes=123 * 2**19
        ),
    )(selected, queries, all_key_states, all_value_states)


def attend_kernel(valid_ref, query_ref, key_ref, value_ref, out_ref):
    rows = query_ref.shape[0]
    causal = lax.broadcasted_iota(jnp.int32, (rows, rows), 1) <= lax.broadcasted_iota(
        jnp.int32, (rows, rows), 0
    )
    out_ref[...] = attend_head(
        query_ref[...],
        key_ref[...],
        with_ones(value_ref[...]),
        causal,
        valid_ref[0] != 0,
        valid_ref[1] != 0,
    )


def exchanged(queries, all_key_states, all_value_states, selected):
    devices = lax.axis_size("ctx")
    me = lax.axis_index("ctx")
    rows, width = all_key_states.shape
    exchange = functools.partial(
        lax.all_to_all, axis_name="ctx", split_axis=0, concat_axis=0, tiled=True
    )
    both = jnp.concatenate([all_key_states, all_value_states], axis=1)
    requests = lax.all_gather(selected, "ctx", axis=0, tiled=True)
    held = exchange(both.reshape(devices, rows // devices, 2 * width))
    flat = held.reshape(devices, rows // devices * 2 * width)
    numbers = jnp.arange(devices, dtype=requests.dtype)

    def picked(choice):
        pick = (requests[:, choice, None] == numbers[None, :]).astype(flat.dtype)
        taken = jnp.dot(pick, flat, preferred_element_type=jnp.float32).astype(flat.dtype)
        return exchange(taken.reshape(held.shape)).reshape(rows, 2 * width)

    chosen = [picked(choice) for choice in range(2)]
    everything = jnp.concatenate([both] + chosen, axis=0)
    first, second = selected[0, 0], selected[0, 1]
    valid = jnp.stack([first < me, jnp.logical_and(second < me, second != first)])
    return pl.pallas_call(
        attend_kernel,
        out_shape=jax.ShapeDtypeStruct(queries.shape, queries.dtype),
        grid=(QUERY_HEADS,),
        in_specs=[
            pl.BlockSpec(memory_space=pltpu.SMEM),
            pl.BlockSpec((rows, HEAD_SIZE), lambda h: (0, h)),
            pl.BlockSpec((3 * rows, HEAD_SIZE), lambda h: (0, h // GROUP_WIDTH)),
            pl.BlockSpec((3 * rows, HEAD_SIZE), lambda h: (0, KEY_VALUE_HEADS + h // GROUP_WIDTH)),
        ],
        out_specs=pl.BlockSpec((rows, HEAD_SIZE), lambda h: (0, h)),
    )(valid.astype(jnp.int32), queries, everything, everything)


def solution(mesh):
    placed = P(("groups", "ctx"), None)
    local = relayed if mesh.shape["ctx"] == LAYERS * SIDE else exchanged
    return jax.shard_map(
        local, mesh=mesh, in_specs=(placed,) * 4, out_specs=placed, check_vma=False
    )
```

```python
import functools
import math

import jax
import jax.numpy as jnp
from jax import lax
from jax.experimental import pallas as pl
from jax.experimental.pallas import tpu as pltpu
from jax.sharding import PartitionSpec as P

QUERY_HEADS = 32
KEY_VALUE_HEADS = 4
HEAD_SIZE = 128
GROUP_WIDTH = QUERY_HEADS // KEY_VALUE_HEADS
EXPONENT_SCALE = math.log2(math.e) / math.sqrt(HEAD_SIZE)
MASKED = -1e30
LAYERS = 4
SIDE = 4
DIRECT = 3
MESH = pl.DeviceIdType.MESH


def half_max(scores):
    return jnp.maximum(scores[:, :HEAD_SIZE], scores[:, HEAD_SIZE:])


def weigh(queries, keys, causal, first_valid, second_valid):
    rows = queries.shape[0]
    scores = lax.dot_general(
        queries, keys, (((1,), (1,)), ((), ())), preferred_element_type=jnp.float32
    )
    own = jnp.where(causal, scores[:, :rows], MASKED)
    first = scores[:, rows : 2 * rows]
    second = scores[:, 2 * rows :]
    row_max = jnp.max(
        jnp.maximum(
            half_max(own),
            jnp.maximum(
                jnp.where(first_valid, half_max(first), MASKED),
                jnp.where(second_valid, half_max(second), MASKED),
            ),
        ),
        axis=1,
        keepdims=True,
    )
    first_max = jnp.where(first_valid, row_max, -MASKED)
    second_max = jnp.where(second_valid, row_max, -MASKED)
    return jnp.concatenate(
        [
            jnp.exp2((part - top) * EXPONENT_SCALE).astype(jnp.bfloat16)
            for part, top in ((own, row_max), (first, first_max), (second, second_max))
        ],
        axis=1,
    )


def mix(weights, values):
    mixture = jnp.dot(weights, values, preferred_element_type=jnp.float32)
    return (mixture[:, :HEAD_SIZE] * (1.0 / mixture[:, HEAD_SIZE:])).astype(jnp.bfloat16)


def attend_head(queries, keys, values, causal, first_valid, second_valid):
    return mix(weigh(queries, keys, causal, first_valid, second_valid), values)


def with_ones(values):
    return jnp.concatenate([values, jnp.ones_like(values)], axis=1)


def causal_mask(rows):
    return lax.broadcasted_iota(jnp.int32, (rows, rows), 1) <= lax.broadcasted_iota(
        jnp.int32, (rows, rows), 0
    )


def relay_kernel(rows, selected_hbm, query_hbm, key_hbm, value_hbm, out_ref, *scratch):
    heads = KEY_VALUE_HEADS
    chunks = 2 * heads
    stores = scratch[:chunks]
    outgoing = scratch[chunks : 2 * chunks]
    gathered = scratch[2 * chunks : 3 * chunks]
    (
        query_ref,
        weight_ref,
        request_vmem,
        request_smem,
        selected_ref,
        local_sem,
        request_send,
        request_recv,
        layer_recv,
        below_recv,
        deliver_recv,
        pass_send,
        deliver_send,
    ) = scratch[3 * chunks :]
    quarter = rows // SIDE
    top = LAYERS - 1
    me = lax.axis_index("ctx")
    layer = me // SIDE
    place = me % SIDE
    mine = pl.ds(place * quarter, quarter)

    def on_layer(*layers):
        wanted = layer == layers[0]
        for other in layers[1:]:
            wanted = jnp.logical_or(wanted, layer == other)
        return pl.when(wanted)

    def peer(offset):
        return layer * SIDE + (place + offset) % SIDE

    def remote(src, dst, send, recv, target):
        return pltpu.make_async_remote_copy(
            src_ref=src,
            dst_ref=dst,
            send_sem=send,
            recv_sem=recv,
            device_id={"ctx": target},
            device_id_type=MESH,
        )

    def stacked(pieces):
        return query_ref.at[pl.ds(0, pieces * quarter * HEAD_SIZE // query_ref.shape[1]), :]

    def pack(c):
        source = (key_hbm, value_hbm)[c % 2]
        return pltpu.make_async_copy(
            source.at[:, pl.ds(c // 2 * HEAD_SIZE, HEAD_SIZE)],
            gathered[c].at[0],
            local_sem.at[1],
        )

    def fetch_queries(g):
        columns = pl.ds(g * GROUP_WIDTH * HEAD_SIZE, GROUP_WIDTH * HEAD_SIZE)
        return pltpu.make_async_copy(
            query_hbm.at[:, columns], query_ref.at[:, columns], local_sem.at[2]
        )

    def request(offset):
        slot = request_vmem.at[place]
        return remote(
            slot, slot, request_send, request_recv.at[0], peer(offset)
        )

    def request_down(q):
        return remote(
            request_vmem.at[place],
            request_vmem.at[SIDE + place],
            request_send,
            request_recv.at[1],
            (top - 1) * SIDE + q,
        )

    def wait_bytes(ref, semaphore):
        pltpu.make_async_copy(ref, ref, semaphore).wait()

    def spread(c, offset):
        target = (place + offset) % SIDE
        return remote(
            gathered[c].at[0, pl.ds(target * quarter, quarter), :],
            stores[c].at[me],
            pass_send,
            layer_recv.at[c],
            peer(offset),
        )

    def direct(c, q):
        return remote(
            gathered[c].at[0, pl.ds(q * quarter, quarter), :],
            stores[c].at[me],
            pass_send,
            below_recv.at[c],
            (layer + 1) % LAYERS * SIDE + q,
        )

    def chain(c, source_layer):
        part = stores[c].at[pl.ds(source_layer * SIDE, SIDE)]
        return remote(
            part,
            part,
            pass_send,
            below_recv.at[c],
            (layer + 1) % LAYERS * SIDE + place,
        )

    def deliver(c, offset):
        return remote(
            outgoing[c].at[offset - 1],
            gathered[c].at[pl.ds(1, 2), mine, :],
            deliver_send,
            deliver_recv.at[c],
            peer(offset),
        )

    def choices_of(q):
        return (1,) if q == SIDE - 1 else (0, 1)

    def deliver_up(c, q):
        span = len(choices_of(q))
        return remote(
            outgoing[c].at[SIDE - 1 + q, pl.ds(2 - span, span)],
            gathered[c].at[pl.ds(3 - span, span), mine, :],
            pass_send,
            deliver_recv.at[c],
            top * SIDE + q,
        )

    def dense(c, source, target, slot, recv):
        return remote(
            gathered[c].at[source],
            gathered[c].at[3 + slot],
            pass_send,
            recv.at[c],
            top * SIDE + target,
        )

    def dense_of(c, q):
        plan = {
            0: ((1, 0, below_recv), (2, 0, layer_recv)),
            1: ((3, 1, layer_recv),),
            2: ((3, 2, below_recv),),
            3: (),
        }[q]
        return [dense(c, 0, *target) for target in plan]

    def relay_of(c, q):
        return dense(c, 3, 3, 0, below_recv) if q == 2 else dense(c, 4, 2, 1, below_recv)

    def on_place(q):
        return pl.when(me == top * SIDE + q)

    fetch_selected = pltpu.make_async_copy(selected_hbm, selected_ref, local_sem.at[0])
    fetch_selected.start()
    for c in range(chunks):
        pack(c).start()
    for g in range(heads):
        fetch_queries(g).start()

    barrier = pltpu.get_barrier_semaphore()
    for offset in range(1, SIDE):
        pl.semaphore_signal(barrier, inc=1, device_id={"ctx": peer(offset)}, device_id_type=MESH)

    @pl.when(layer > 0)
    def _():
        for q in range(SIDE):
            pl.semaphore_signal(
                barrier, inc=1, device_id={"ctx": (layer - 1) * SIDE + q}, device_id_type=MESH
            )

    @pl.when(layer < top)
    def _():
        for q in range(SIDE):
            pl.semaphore_signal(
                barrier, inc=1, device_id={"ctx": (layer + 1) * SIDE + q}, device_id_type=MESH
            )

    neighbour_layers = jnp.minimum(layer, 1) + jnp.minimum(top - layer, 1)
    pl.semaphore_wait(barrier, SIDE - 1 + SIDE * neighbour_layers)

    fetch_selected.wait()
    lane = lax.broadcasted_iota(jnp.int32, (1, 128), 1)
    request_vmem[place] = jnp.where(lane == 0, selected_ref[0, 0], selected_ref[0, 1])

    @on_layer(top)
    def _():
        for q in range(SIDE):
            request_down(q).start()

    @pl.when(layer < top)
    def _():
        for offset in range(1, SIDE):
            request(offset).start()

    wait_bytes(stacked(chunks * 4), local_sem.at[1])
    for c in range(chunks):
        if c < DIRECT:

            @on_layer(0, 1)
            def _():
                for q in range(SIDE):
                    direct(c, q).start()

        @pl.when(layer < top)
        def _():
            for offset in range(1, SIDE):
                spread(c, offset).start()
            stores[c][me] = gathered[c][0, mine, :]

        for q in range(SIDE - 1):

            @on_place(q)
            def _():
                for copy in dense_of(c, q):
                    copy.start()

    first_valid = selected_ref[0, 0] < me
    second_valid = jnp.logical_and(
        selected_ref[0, 1] < me, selected_ref[0, 1] != selected_ref[0, 0]
    )
    causal = causal_mask(rows)

    def slot_of(choice):
        wanted = selected_ref[0, choice]
        local = jnp.logical_and(layer == top, wanted >= top * SIDE)
        return jnp.where(local, 3 + wanted - top * SIDE, 1 + choice)

    def three(c):
        return jnp.concatenate(
            [gathered[c][0], gathered[c][slot_of(0)], gathered[c][slot_of(1)]], axis=0
        )

    def wait_pieces(c, pieces, semaphore):
        wait_bytes(stores[c].at[pl.ds(0, pieces)], semaphore.at[c])

    @pl.when(layer < top)
    def _():
        wait_bytes(request_vmem.at[pl.ds(0, SIDE - 1)], request_recv.at[0])

    @on_layer(top - 1)
    def _():
        wait_bytes(request_vmem.at[pl.ds(0, SIDE)], request_recv.at[1])

    @pl.when(layer != top - 1)
    def _():
        for q in range(SIDE):
            request_vmem[SIDE + q] = jnp.zeros((1, 128), jnp.int32)

    @on_layer(top)
    def _():
        for offset in range(1, SIDE):
            request_vmem[(place + offset) % SIDE] = jnp.zeros((1, 128), jnp.int32)

    to_smem = pltpu.make_async_copy(request_vmem, request_smem, local_sem.at[0])
    to_smem.start()
    to_smem.wait()

    def hand_out(c):
        for offset in range(1, SIDE):
            for choice in range(2):
                wanted = request_smem[(place + offset) % SIDE, 0, choice]
                outgoing[c][offset - 1, choice] = stores[c][wanted]
            deliver(c, offset).start()
        for choice in range(2):
            gathered[c][1 + choice, mine, :] = stores[c][request_smem[place, 0, choice]]

    def hand_up(c):
        for q in range(SIDE):
            for choice in choices_of(q):
                wanted = jnp.minimum(request_smem[SIDE + q, 0, choice], top * SIDE - 1)
                outgoing[c][SIDE - 1 + q, choice] = stores[c][wanted]
            deliver_up(c, q).start()

    def serve_bottom(c):
        wait_pieces(c, SIDE - 1, layer_recv)
        if c >= DIRECT:
            chain(c, 0).start()
        hand_out(c)

    def serve_second(c):
        wait_pieces(c, SIDE, below_recv)
        chain(c, 0).start()
        if c == 0:
            for early in range(DIRECT):
                wait_pieces(early, SIDE - 1, layer_recv)
        if DIRECT <= c + 1 < chunks:
            wait_pieces(c + 1, SIDE - 1, layer_recv)
            chain(c + 1, 1).start()
        hand_out(c)

    def serve_third(c):
        wait_pieces(c, SIDE - 1, layer_recv)
        wait_pieces(c, 2 * SIDE, below_recv)
        hand_up(c)
        hand_out(c)

    def serve_top(c):
        @pl.when(place >= 2)
        def _():
            wait_pieces(c, SIDE, layer_recv)

        for q in (2, 3):

            @on_place(q)
            def _():
                relay_of(c, q).start()

    def serve(step):
        for number, (work, ahead) in enumerate(
            ((serve_bottom, chunks), (serve_second, 3), (serve_third, 0), (serve_top, 3))
        ):
            begin = 0 if step == 0 else min(step + ahead, chunks)
            end = min(step + ahead + 1, chunks)
            if begin < end:

                @on_layer(number)
                def _():
                    for c in range(begin, end):
                        work(c)

    def wait_delivery(c):
        @pl.when(layer < top)
        def _():
            wait_pieces(c, 2 * (SIDE - 1), deliver_recv)

        for q in range(SIDE):

            @on_place(q)
            def _():
                wait_pieces(c, SIDE * len(choices_of(q)), deliver_recv)
                if q > 0:
                    wait_pieces(c, SIDE * (2 if q == 3 else 1), below_recv)

    def compute(c):
        wait_delivery(c)
        g = c // 2
        if c % 2 == 0:
            if g == 0:
                wait_bytes(query_ref, local_sem.at[2])
            keys = three(c)
            for index in range(GROUP_WIDTH):
                columns = pl.ds((g * GROUP_WIDTH + index) * HEAD_SIZE, HEAD_SIZE)
                weight_ref[index] = weigh(
                    query_ref[:, columns], keys, causal, first_valid, second_valid
                )
        else:
            values = with_ones(three(c))
            for index in range(GROUP_WIDTH):
                columns = pl.ds((g * GROUP_WIDTH + index) * HEAD_SIZE, HEAD_SIZE)
                out_ref[:, columns] = mix(weight_ref[index], values)

    for step in range(chunks):
        serve(step)
        if step > 0:
            compute(step - 1)
    compute(chunks - 1)

    within = chunks * (SIDE - 1)
    first = DIRECT * SIDE
    own = (chunks - DIRECT) * SIDE
    passed = (
        within + first + own,
        within + first + own + chunks * SIDE,
        within + chunks * (2 * SIDE - 1),
    )
    for number, pieces in enumerate(passed):

        @on_layer(number)
        def _():
            wait_bytes(stacked(pieces), pass_send)
            wait_bytes(weight_ref.at[pl.ds(0, 2)], deliver_send)
            wait_bytes(request_vmem.at[pl.ds(0, SIDE - 1)], request_send)

    @on_layer(top)
    def _():
        wait_bytes(request_vmem.at[pl.ds(0, SIDE)], request_send)

    for q, blocks in enumerate((2, 1, 2, 1)):

        @on_place(q)
        def _():
            wait_bytes(stacked(chunks * blocks * SIDE), pass_send)


def relayed(queries, all_key_states, all_value_states, selected):
    rows = queries.shape[0]
    quarter = rows // SIDE
    chunks = 2 * KEY_VALUE_HEADS
    blocks = LAYERS * SIDE
    kind = all_key_states.dtype
    dma = pltpu.SemaphoreType.DMA
    return pl.pallas_call(
        functools.partial(relay_kernel, rows),
        out_shape=pltpu.VMEM(queries.shape, queries.dtype),
        in_specs=[pl.BlockSpec(memory_space=pltpu.HBM)] * 4,
        out_specs=pl.BlockSpec(memory_space=pltpu.VMEM),
        scratch_shapes=[pltpu.VMEM((blocks, quarter, HEAD_SIZE), kind)] * chunks
        + [pltpu.VMEM((2 * SIDE - 1, 2, quarter, HEAD_SIZE), kind)] * chunks
        + [pltpu.VMEM((6, rows, HEAD_SIZE), kind)] * chunks
        + [
            pltpu.VMEM(queries.shape, queries.dtype),
            pltpu.VMEM((GROUP_WIDTH, rows, 3 * rows), kind),
            pltpu.VMEM((2 * SIDE, 1, 128), jnp.int32),
            pltpu.SMEM((2 * SIDE, 1, 128), jnp.int32),
            pltpu.SMEM((1, 2), jnp.int32),
            dma((3,)),
            dma,
            dma((2,)),
            dma((chunks,)),
            dma((chunks,)),
            dma((chunks,)),
            dma,
            dma,
        ],
        compiler_params=pltpu.CompilerParams(
            collective_id=0, has_side_effects=True, vmem_limit_bytes=123 * 2**19
        ),
    )(selected, queries, all_key_states, all_value_states)


def attend_kernel(valid_ref, query_ref, key_ref, value_ref, out_ref):
    rows = query_ref.shape[0]
    causal = lax.broadcasted_iota(jnp.int32, (rows, rows), 1) <= lax.broadcasted_iota(
        jnp.int32, (rows, rows), 0
    )
    out_ref[...] = attend_head(
        query_ref[...],
        key_ref[...],
        with_ones(value_ref[...]),
        causal,
        valid_ref[0] != 0,
        valid_ref[1] != 0,
    )


def exchanged(queries, all_key_states, all_value_states, selected):
    devices = lax.axis_size("ctx")
    me = lax.axis_index("ctx")
    rows, width = all_key_states.shape
    exchange = functools.partial(
        lax.all_to_all, axis_name="ctx", split_axis=0, concat_axis=0, tiled=True
    )
    both = jnp.concatenate([all_key_states, all_value_states], axis=1)
    requests = lax.all_gather(selected, "ctx", axis=0, tiled=True)
    held = exchange(both.reshape(devices, rows // devices, 2 * width))
    flat = held.reshape(devices, rows // devices * 2 * width)
    numbers = jnp.arange(devices, dtype=requests.dtype)

    def picked(choice):
        pick = (requests[:, choice, None] == numbers[None, :]).astype(flat.dtype)
        taken = jnp.dot(pick, flat, preferred_element_type=jnp.float32).astype(flat.dtype)
        return exchange(taken.reshape(held.shape)).reshape(rows, 2 * width)

    chosen = [picked(choice) for choice in range(2)]
    everything = jnp.concatenate([both] + chosen, axis=0)
    first, second = selected[0, 0], selected[0, 1]
    valid = jnp.stack([first < me, jnp.logical_and(second < me, second != first)])
    return pl.pallas_call(
        attend_kernel,
        out_shape=jax.ShapeDtypeStruct(queries.shape, queries.dtype),
        grid=(QUERY_HEADS,),
        in_specs=[
            pl.BlockSpec(memory_space=pltpu.SMEM),
            pl.BlockSpec((rows, HEAD_SIZE), lambda h: (0, h)),
            pl.BlockSpec((3 * rows, HEAD_SIZE), lambda h: (0, h // GROUP_WIDTH)),
            pl.BlockSpec((3 * rows, HEAD_SIZE), lambda h: (0, KEY_VALUE_HEADS + h // GROUP_WIDTH)),
        ],
        out_specs=pl.BlockSpec((rows, HEAD_SIZE), lambda h: (0, h)),
    )(valid.astype(jnp.int32), queries, everything, everything)


def solution(mesh):
    placed = P(("groups", "ctx"), None)
    local = relayed if mesh.shape["ctx"] == LAYERS * SIDE else exchanged
    return jax.shard_map(
        local, mesh=mesh, in_specs=(placed,) * 4, out_specs=placed, check_vma=False
    )
```

```python
import functools
import math

import jax
import jax.numpy as jnp
from jax import lax
from jax.experimental import pallas as pl
from jax.experimental.pallas import tpu as pltpu
from jax.sharding import PartitionSpec as P

QUERY_HEADS = 32
KEY_VALUE_HEADS = 4
HEAD_SIZE = 128
GROUP_WIDTH = QUERY_HEADS // KEY_VALUE_HEADS
EXPONENT_SCALE = math.log2(math.e) / math.sqrt(HEAD_SIZE)
MASKED = -1e30
LAYERS = 4
SIDE = 4
DIRECT = 3
AHEAD = 2
SERVED = (
    (0, 17, 17, 17, 17, 17, 17, 17, 17, 17),
    (0, 7, 9, 13, 17, 17, 17, 17, 17, 17),
    (0, 3, 4, 5, 7, 9, 11, 13, 15, 17),
    (0, 3, 5, 9, 17, 17, 17, 17, 17, 17),
)
MESH = pl.DeviceIdType.MESH


def half_max(scores):
    return jnp.maximum(scores[:, :HEAD_SIZE], scores[:, HEAD_SIZE:])


def weigh(queries, keys, causal, first_valid, second_valid):
    rows = queries.shape[0]
    scores = lax.dot_general(
        queries, keys, (((1,), (1,)), ((), ())), preferred_element_type=jnp.float32
    )
    own = jnp.where(causal, scores[:, :rows], MASKED)
    first = scores[:, rows : 2 * rows]
    second = scores[:, 2 * rows :]
    row_max = jnp.max(
        jnp.maximum(
            half_max(own),
            jnp.maximum(
                jnp.where(first_valid, half_max(first), MASKED),
                jnp.where(second_valid, half_max(second), MASKED),
            ),
        ),
        axis=1,
        keepdims=True,
    )
    first_max = jnp.where(first_valid, row_max, -MASKED)
    second_max = jnp.where(second_valid, row_max, -MASKED)
    return jnp.concatenate(
        [
            jnp.exp2((part - top) * EXPONENT_SCALE).astype(jnp.bfloat16)
            for part, top in ((own, row_max), (first, first_max), (second, second_max))
        ],
        axis=1,
    )


def normalised(mixture):
    return (mixture[:, :HEAD_SIZE] * (1.0 / mixture[:, HEAD_SIZE:])).astype(jnp.bfloat16)


def mix(weights, values):
    return normalised(jnp.dot(weights, values, preferred_element_type=jnp.float32))


def attend_head(queries, keys, values, causal, first_valid, second_valid):
    return mix(weigh(queries, keys, causal, first_valid, second_valid), values)


def with_ones(values):
    return jnp.concatenate([values, jnp.ones_like(values)], axis=1)


def causal_mask(rows):
    return lax.broadcasted_iota(jnp.int32, (rows, rows), 1) <= lax.broadcasted_iota(
        jnp.int32, (rows, rows), 0
    )


def parts_of(rows):
    order = ((0, 0, 1), (1, 0, 1), (0, 1, 1), (1, 1, 2), (0, 2, 2), (0, 3, 2), (1, 2, 4), (1, 3, 4))
    return [
        (kind, g, rows // cuts * i, rows // cuts) for kind, g, cuts in order for i in range(cuts)
    ]


def relay_kernel(rows, selected_hbm, query_hbm, key_hbm, value_hbm, out_ref, *scratch):
    heads = KEY_VALUE_HEADS
    parts = parts_of(rows)
    chunks = len(parts)
    stores = scratch[:chunks]
    outgoing = scratch[chunks : 2 * chunks]
    gathered = scratch[2 * chunks : 3 * chunks]
    (
        query_ref,
        weight_ref,
        total_ref,
        request_vmem,
        request_smem,
        selected_ref,
        local_sem,
        request_send,
        request_recv,
        layer_recv,
        below_recv,
        deliver_recv,
        pass_send,
        deliver_send,
    ) = scratch[3 * chunks :]
    unit = rows // SIDE
    top = LAYERS - 1
    me = lax.axis_index("ctx")
    layer = me // SIDE
    place = me % SIDE

    def quarter_of(c, q):
        size = parts[c][3] // SIDE
        return pl.ds(q * size, size)

    def on_layer(*layers):
        wanted = layer == layers[0]
        for other in layers[1:]:
            wanted = jnp.logical_or(wanted, layer == other)
        return pl.when(wanted)

    def peer(offset):
        return layer * SIDE + (place + offset) % SIDE

    def remote(src, dst, send, recv, target):
        return pltpu.make_async_remote_copy(
            src_ref=src,
            dst_ref=dst,
            send_sem=send,
            recv_sem=recv,
            device_id={"ctx": target},
            device_id_type=MESH,
        )

    def stacked(pieces):
        return query_ref.at[pl.ds(0, pieces * unit * HEAD_SIZE // query_ref.shape[1]), :]

    def pack(c):
        kind, g, start, count = parts[c]
        return pltpu.make_async_copy(
            (key_hbm, value_hbm)[kind].at[pl.ds(start, count), pl.ds(g * HEAD_SIZE, HEAD_SIZE)],
            gathered[c].at[0],
            local_sem.at[1],
        )

    def fetch_queries(g):
        columns = pl.ds(g * GROUP_WIDTH * HEAD_SIZE, GROUP_WIDTH * HEAD_SIZE)
        return pltpu.make_async_copy(
            query_hbm.at[:, columns], query_ref.at[:, columns], local_sem.at[2]
        )

    def request(offset):
        slot = request_vmem.at[place]
        return remote(
            slot, slot, request_send, request_recv.at[0], peer(offset)
        )

    def request_down(q):
        return remote(
            request_vmem.at[place],
            request_vmem.at[SIDE + place],
            request_send,
            request_recv.at[1],
            (top - 1) * SIDE + q,
        )

    def wait_bytes(ref, semaphore):
        pltpu.make_async_copy(ref, ref, semaphore).wait()

    def spread(c, offset):
        target = (place + offset) % SIDE
        return remote(
            gathered[c].at[0, quarter_of(c, target), :],
            stores[c].at[me],
            pass_send,
            layer_recv.at[c],
            peer(offset),
        )

    def direct(c, q):
        return remote(
            gathered[c].at[0, quarter_of(c, q), :],
            stores[c].at[me],
            pass_send,
            below_recv.at[c],
            (layer + 1) % LAYERS * SIDE + q,
        )

    def chain(c, source_layer):
        part = stores[c].at[pl.ds(source_layer * SIDE, SIDE)]
        return remote(
            part,
            part,
            pass_send,
            below_recv.at[c],
            (layer + 1) % LAYERS * SIDE + place,
        )

    def deliver(c, offset):
        return remote(
            outgoing[c].at[offset - 1],
            gathered[c].at[pl.ds(1, 2), quarter_of(c, place), :],
            deliver_send,
            deliver_recv.at[c],
            peer(offset),
        )

    def choices_of(q):
        return (1,) if q == SIDE - 1 else (0, 1)

    def deliver_up(c, q):
        span = len(choices_of(q))
        return remote(
            outgoing[c].at[SIDE - 1 + q, pl.ds(2 - span, span)],
            gathered[c].at[pl.ds(3 - span, span), quarter_of(c, place), :],
            pass_send,
            deliver_recv.at[c],
            top * SIDE + q,
        )

    def dense(c, source, target, slot, recv):
        return remote(
            gathered[c].at[source],
            gathered[c].at[3 + slot],
            pass_send,
            recv.at[c],
            top * SIDE + target,
        )

    def dense_of(c, q):
        plan = {
            0: ((1, 0, below_recv), (2, 0, layer_recv)),
            1: ((3, 1, layer_recv),),
            2: ((3, 2, below_recv),),
            3: (),
        }[q]
        return [dense(c, 0, *target) for target in plan]

    def relay_of(c, q):
        return dense(c, 3, 3, 0, below_recv) if q == 2 else dense(c, 4, 2, 1, below_recv)

    def on_place(q):
        return pl.when(me == top * SIDE + q)

    fetch_selected = pltpu.make_async_copy(selected_hbm, selected_ref, local_sem.at[0])
    fetch_selected.start()
    for c in range(chunks):
        pack(c).start()
    for g in range(heads):
        fetch_queries(g).start()

    barrier = pltpu.get_barrier_semaphore()
    for offset in range(1, SIDE):
        pl.semaphore_signal(barrier, inc=1, device_id={"ctx": peer(offset)}, device_id_type=MESH)

    @pl.when(layer > 0)
    def _():
        for q in range(SIDE):
            pl.semaphore_signal(
                barrier, inc=1, device_id={"ctx": (layer - 1) * SIDE + q}, device_id_type=MESH
            )

    @pl.when(layer < top)
    def _():
        for q in range(SIDE):
            pl.semaphore_signal(
                barrier, inc=1, device_id={"ctx": (layer + 1) * SIDE + q}, device_id_type=MESH
            )

    neighbour_layers = jnp.minimum(layer, 1) + jnp.minimum(top - layer, 1)
    pl.semaphore_wait(barrier, SIDE - 1 + SIDE * neighbour_layers)

    wait_bytes(stacked(2 * heads * SIDE), local_sem.at[1])

    @on_layer(0, 1)
    def _():
        for c in range(AHEAD):
            for q in range(SIDE):
                direct(c, q).start()

    @on_layer(0)
    def _():
        for c in range(AHEAD, DIRECT):
            for q in range(SIDE):
                direct(c, q).start()

    fetch_selected.wait()
    lane = lax.broadcasted_iota(jnp.int32, (1, 128), 1)
    request_vmem[place] = jnp.where(lane == 0, selected_ref[0, 0], selected_ref[0, 1])

    @on_layer(top)
    def _():
        for q in range(SIDE):
            request_down(q).start()

    @pl.when(layer < top)
    def _():
        for offset in range(1, SIDE):
            request(offset).start()

    for c in range(chunks):
        @pl.when(layer < top)
        def _():
            for offset in range(1, SIDE):
                spread(c, offset).start()
            stores[c][me] = gathered[c][0, quarter_of(c, place), :]

        for q in range(SIDE - 1):

            @on_place(q)
            def _():
                for copy in dense_of(c, q):
                    copy.start()

    first_valid = selected_ref[0, 0] < me
    second_valid = jnp.logical_and(
        selected_ref[0, 1] < me, selected_ref[0, 1] != selected_ref[0, 0]
    )
    causal = causal_mask(rows)

    def slot_of(choice):
        wanted = selected_ref[0, choice]
        local = jnp.logical_and(layer == top, wanted >= top * SIDE)
        return jnp.where(local, 3 + wanted - top * SIDE, 1 + choice)

    def rows_from(c, slot):
        return gathered[c][slot_of(slot - 1) if slot else 0]

    def wait_pieces(c, pieces, semaphore):
        wait_bytes(stores[c].at[pl.ds(0, pieces)], semaphore.at[c])

    @on_layer(1)
    def _():
        for c in range(AHEAD):
            wait_pieces(c, SIDE, below_recv)
            chain(c, 0).start()
        for c in range(AHEAD, DIRECT):
            for q in range(SIDE):
                direct(c, q).start()

    @pl.when(layer < top)
    def _():
        wait_bytes(request_vmem.at[pl.ds(0, SIDE - 1)], request_recv.at[0])

    @on_layer(top - 1)
    def _():
        wait_bytes(request_vmem.at[pl.ds(0, SIDE)], request_recv.at[1])

    @pl.when(layer != top - 1)
    def _():
        for q in range(SIDE):
            request_vmem[SIDE + q] = jnp.zeros((1, 128), jnp.int32)

    @on_layer(top)
    def _():
        for offset in range(1, SIDE):
            request_vmem[(place + offset) % SIDE] = jnp.zeros((1, 128), jnp.int32)

    to_smem = pltpu.make_async_copy(request_vmem, request_smem, local_sem.at[0])
    to_smem.start()
    to_smem.wait()

    def hand_out(c):
        for offset in range(1, SIDE):
            for choice in range(2):
                wanted = request_smem[(place + offset) % SIDE, 0, choice]
                outgoing[c][offset - 1, choice] = stores[c][wanted]
            deliver(c, offset).start()
        for choice in range(2):
            gathered[c][1 + choice, quarter_of(c, place), :] = stores[c][request_smem[place, 0, choice]]

    def hand_up(c):
        for q in range(SIDE):
            for choice in choices_of(q):
                wanted = jnp.minimum(request_smem[SIDE + q, 0, choice], top * SIDE - 1)
                outgoing[c][SIDE - 1 + q, choice] = stores[c][wanted]
            deliver_up(c, q).start()

    def serve_bottom(c):
        wait_pieces(c, SIDE - 1, layer_recv)
        if c >= DIRECT:
            chain(c, 0).start()
        hand_out(c)

    def serve_second(c):
        if c >= AHEAD:
            wait_pieces(c, SIDE, below_recv)
            chain(c, 0).start()
        if c == 0:
            for early in range(DIRECT):
                wait_pieces(early, SIDE - 1, layer_recv)
        if DIRECT <= c + 1 < chunks:
            wait_pieces(c + 1, SIDE - 1, layer_recv)
            chain(c + 1, 1).start()
        hand_out(c)

    def serve_third(c):
        wait_pieces(c, SIDE - 1, layer_recv)
        wait_pieces(c, 2 * SIDE, below_recv)
        hand_up(c)
        hand_out(c)

    def serve_top(c):
        @pl.when(place >= 2)
        def _():
            wait_pieces(c, SIDE, layer_recv)

        for q in (2, 3):

            @on_place(q)
            def _():
                relay_of(c, q).start()

    def serve(step):
        works = (serve_bottom, serve_second, serve_third, serve_top)
        for number, (work, plan) in enumerate(zip(works, SERVED)):
            if plan[step] < plan[step + 1]:

                @on_layer(number)
                def _():
                    for c in range(plan[step], plan[step + 1]):
                        work(c)

    def wait_delivery(c):
        @pl.when(layer < top)
        def _():
            wait_pieces(c, 2 * (SIDE - 1), deliver_recv)

        for q in range(SIDE):

            @on_place(q)
            def _():
                wait_pieces(c, SIDE * len(choices_of(q)), deliver_recv)
                if q > 0:
                    wait_pieces(c, SIDE * (2 if q == 3 else 1), below_recv)

    def head_columns(g, index):
        return pl.ds((g * GROUP_WIDTH + index) * HEAD_SIZE, HEAD_SIZE)

    def weigh_group(run, heads_of=range(GROUP_WIDTH)):
        if heads_of[0] == 0:
            for c in run:
                wait_delivery(c)
        g = parts[run[0]][1]
        keys = jnp.concatenate([rows_from(c, slot) for slot in range(3) for c in run], axis=0)
        for index in heads_of:
            weight_ref[g % 2 * GROUP_WIDTH + index] = weigh(
                query_ref[:, head_columns(g, index)], keys, causal, first_valid, second_valid
            )

    def mix_group(arriving, runs, begins=True, ends=True):
        for c in arriving:
            wait_delivery(c)
        g = parts[arriving[0]][1]
        values = with_ones(
            jnp.concatenate([rows_from(c, slot) for slot, run in runs for c in run], axis=0)
        )
        for index in range(GROUP_WIDTH):
            weights = jnp.concatenate(
                [
                    weight_ref[
                        g % 2 * GROUP_WIDTH + index,
                        :,
                        pl.ds(slot * rows + parts[run[0]][2], sum(parts[c][3] for c in run)),
                    ]
                    for slot, run in runs
                ],
                axis=1,
            )
            mixture = jnp.dot(weights, values, preferred_element_type=jnp.float32)
            if not begins:
                mixture += total_ref[index]
            if ends:
                out_ref[:, head_columns(g, index)] = normalised(mixture)
            else:
                total_ref[index] = mixture

    def mix_whole(*run):
        mix_group(run, [(slot, run) for slot in range(3)])

    low, high = range(GROUP_WIDTH // 2), range(GROUP_WIDTH // 2, GROUP_WIDTH)
    serve(0)
    wait_bytes(query_ref, local_sem.at[2])
    weigh_group((0,))
    serve(1)
    mix_whole(1)
    serve(2)
    weigh_group((2,))
    serve(3)
    mix_whole(3, 4)
    serve(4)
    weigh_group((5, 6), low)
    serve(5)
    weigh_group((5, 6), high)
    serve(6)
    weigh_group((7, 8), low)
    serve(7)
    weigh_group((7, 8), high)
    serve(8)
    mix_whole(9, 10, 11, 12)
    mix_group((13, 14), [(0, (13, 14, 15, 16)), (1, (13, 14)), (2, (13, 14))], ends=False)
    mix_group((15, 16), [(1, (15, 16)), (2, (15, 16))], begins=False)

    full = 2 * heads
    within = full * (SIDE - 1)
    passed = (
        within + full * SIDE,
        within + full * SIDE + full * SIDE,
        within + full * (2 * SIDE - 1),
    )
    for number, pieces in enumerate(passed):

        @on_layer(number)
        def _():
            wait_bytes(stacked(pieces), pass_send)
            wait_bytes(weight_ref.at[pl.ds(0, 2)], deliver_send)
            wait_bytes(request_vmem.at[pl.ds(0, SIDE - 1)], request_send)

    @on_layer(top)
    def _():
        wait_bytes(request_vmem.at[pl.ds(0, SIDE)], request_send)

    for q, blocks in enumerate((2, 1, 2, 1)):

        @on_place(q)
        def _():
            wait_bytes(stacked(full * blocks * SIDE), pass_send)


def relayed(queries, all_key_states, all_value_states, selected):
    rows = queries.shape[0]
    counts = [count for _, _, _, count in parts_of(rows)]
    chunks = len(counts)
    blocks = LAYERS * SIDE
    kind = all_key_states.dtype
    dma = pltpu.SemaphoreType.DMA
    return pl.pallas_call(
        functools.partial(relay_kernel, rows),
        out_shape=pltpu.VMEM(queries.shape, queries.dtype),
        in_specs=[pl.BlockSpec(memory_space=pltpu.HBM)] * 4,
        out_specs=pl.BlockSpec(memory_space=pltpu.VMEM),
        scratch_shapes=[pltpu.VMEM((blocks, n // SIDE, HEAD_SIZE), kind) for n in counts]
        + [pltpu.VMEM((2 * SIDE - 1, 2, n // SIDE, HEAD_SIZE), kind) for n in counts]
        + [pltpu.VMEM((6, n, HEAD_SIZE), kind) for n in counts]
        + [
            pltpu.VMEM(queries.shape, queries.dtype),
            pltpu.VMEM((2 * GROUP_WIDTH, rows, 3 * rows), kind),
            pltpu.VMEM((GROUP_WIDTH, rows, 2 * HEAD_SIZE), jnp.float32),
            pltpu.VMEM((2 * SIDE, 1, 128), jnp.int32),
            pltpu.SMEM((2 * SIDE, 1, 128), jnp.int32),
            pltpu.SMEM((1, 2), jnp.int32),
            dma((3,)),
            dma,
            dma((2,)),
            dma((chunks,)),
            dma((chunks,)),
            dma((chunks,)),
            dma,
            dma,
        ],
        compiler_params=pltpu.CompilerParams(
            collective_id=0, has_side_effects=True, vmem_limit_bytes=123 * 2**19
        ),
    )(selected, queries, all_key_states, all_value_states)


def attend_kernel(valid_ref, query_ref, key_ref, value_ref, out_ref):
    rows = query_ref.shape[0]
    causal = lax.broadcasted_iota(jnp.int32, (rows, rows), 1) <= lax.broadcasted_iota(
        jnp.int32, (rows, rows), 0
    )
    out_ref[...] = attend_head(
        query_ref[...],
        key_ref[...],
        with_ones(value_ref[...]),
        causal,
        valid_ref[0] != 0,
        valid_ref[1] != 0,
    )


def exchanged(queries, all_key_states, all_value_states, selected):
    devices = lax.axis_size("ctx")
    me = lax.axis_index("ctx")
    rows, width = all_key_states.shape
    exchange = functools.partial(
        lax.all_to_all, axis_name="ctx", split_axis=0, concat_axis=0, tiled=True
    )
    both = jnp.concatenate([all_key_states, all_value_states], axis=1)
    requests = lax.all_gather(selected, "ctx", axis=0, tiled=True)
    held = exchange(both.reshape(devices, rows // devices, 2 * width))
    flat = held.reshape(devices, rows // devices * 2 * width)
    numbers = jnp.arange(devices, dtype=requests.dtype)

    def picked(choice):
        pick = (requests[:, choice, None] == numbers[None, :]).astype(flat.dtype)
        taken = jnp.dot(pick, flat, preferred_element_type=jnp.float32).astype(flat.dtype)
        return exchange(taken.reshape(held.shape)).reshape(rows, 2 * width)

    chosen = [picked(choice) for choice in range(2)]
    everything = jnp.concatenate([both] + chosen, axis=0)
    first, second = selected[0, 0], selected[0, 1]
    valid = jnp.stack([first < me, jnp.logical_and(second < me, second != first)])
    return pl.pallas_call(
        attend_kernel,
        out_shape=jax.ShapeDtypeStruct(queries.shape, queries.dtype),
        grid=(QUERY_HEADS,),
        in_specs=[
            pl.BlockSpec(memory_space=pltpu.SMEM),
            pl.BlockSpec((rows, HEAD_SIZE), lambda h: (0, h)),
            pl.BlockSpec((3 * rows, HEAD_SIZE), lambda h: (0, h // GROUP_WIDTH)),
            pl.BlockSpec((3 * rows, HEAD_SIZE), lambda h: (0, KEY_VALUE_HEADS + h // GROUP_WIDTH)),
        ],
        out_specs=pl.BlockSpec((rows, HEAD_SIZE), lambda h: (0, h)),
    )(valid.astype(jnp.int32), queries, everything, everything)


def solution(mesh):
    placed = P(("groups", "ctx"), None)
    local = relayed if mesh.shape["ctx"] == LAYERS * SIDE else exchanged
    return jax.shard_map(
        local, mesh=mesh, in_specs=(placed,) * 4, out_specs=placed, check_vma=False
    )
```

```python
import functools
import math

import jax
import jax.numpy as jnp
from jax import lax
from jax.experimental import pallas as pl
from jax.experimental.pallas import tpu as pltpu
from jax.sharding import PartitionSpec as P

QUERY_HEADS = 32
KEY_VALUE_HEADS = 4
HEAD_SIZE = 128
GROUP_WIDTH = QUERY_HEADS // KEY_VALUE_HEADS
EXPONENT_SCALE = math.log2(math.e) / math.sqrt(HEAD_SIZE)
MASKED = -1e30
LAYERS = 4
SIDE = 4
DIRECT = 6
AHEAD = 4
SERVED = (
    (0, 20, 20, 20, 20, 20, 20, 20, 20, 20),
    (0, 10, 12, 16, 20, 20, 20, 20, 20, 20),
    (0, 7, 8, 9, 11, 13, 15, 17, 20, 20),
    (0, 6, 8, 12, 20, 20, 20, 20, 20, 20),
)
GROUPS = (2, 2, 2, 2, 2, 2, 4, 2, 2)
MESH = pl.DeviceIdType.MESH


def half_max(scores):
    return jnp.maximum(scores[:, :HEAD_SIZE], scores[:, HEAD_SIZE:])


def weigh(queries, keys, causal, first_valid, second_valid):
    rows = queries.shape[0]
    scores = lax.dot_general(
        queries, keys, (((1,), (1,)), ((), ())), preferred_element_type=jnp.float32
    )
    own = jnp.where(causal, scores[:, :rows], MASKED)
    first = scores[:, rows : 2 * rows]
    second = scores[:, 2 * rows :]
    row_max = jnp.max(
        jnp.maximum(
            half_max(own),
            jnp.maximum(
                jnp.where(first_valid, half_max(first), MASKED),
                jnp.where(second_valid, half_max(second), MASKED),
            ),
        ),
        axis=1,
        keepdims=True,
    )
    first_max = jnp.where(first_valid, row_max, -MASKED)
    second_max = jnp.where(second_valid, row_max, -MASKED)
    return jnp.concatenate(
        [
            jnp.exp2((part - top) * EXPONENT_SCALE).astype(jnp.bfloat16)
            for part, top in ((own, row_max), (first, first_max), (second, second_max))
        ],
        axis=1,
    )


def normalised(mixture):
    return (mixture[:, :HEAD_SIZE] * (1.0 / mixture[:, HEAD_SIZE:])).astype(jnp.bfloat16)


def mix(weights, values):
    return normalised(jnp.dot(weights, values, preferred_element_type=jnp.float32))


def attend_head(queries, keys, values, causal, first_valid, second_valid):
    return mix(weigh(queries, keys, causal, first_valid, second_valid), values)


def with_ones(values):
    return jnp.concatenate([values, jnp.ones_like(values)], axis=1)


def causal_mask(rows):
    return lax.broadcasted_iota(jnp.int32, (rows, rows), 1) <= lax.broadcasted_iota(
        jnp.int32, (rows, rows), 0
    )


def parts_of(rows):
    order = ((0, 0, 2), (1, 0, 2), (0, 1, 2), (1, 1, 2), (0, 2, 2), (0, 3, 2), (1, 2, 4), (1, 3, 4))
    return [
        (kind, g, rows // cuts * i, rows // cuts) for kind, g, cuts in order for i in range(cuts)
    ]


def relay_kernel(rows, selected_hbm, query_hbm, key_hbm, value_hbm, out_ref, *scratch):
    heads = KEY_VALUE_HEADS
    parts = parts_of(rows)
    chunks = len(parts)
    together = [k for k, count in enumerate(GROUPS) for _ in range(count)]
    stores = scratch[:chunks]
    outgoing = scratch[chunks : 2 * chunks]
    gathered = scratch[2 * chunks : 3 * chunks]
    (
        query_ref,
        weight_ref,
        total_ref,
        request_vmem,
        request_smem,
        selected_ref,
        local_sem,
        request_send,
        request_recv,
        layer_recv,
        below_recv,
        deliver_recv,
        pass_send,
        deliver_send,
    ) = scratch[3 * chunks :]
    unit = rows // SIDE
    top = LAYERS - 1
    me = lax.axis_index("ctx")
    layer = me // SIDE
    place = me % SIDE

    def quarter_of(c, q):
        size = parts[c][3] // SIDE
        return pl.ds(q * size, size)

    def on_layer(*layers):
        wanted = layer == layers[0]
        for other in layers[1:]:
            wanted = jnp.logical_or(wanted, layer == other)
        return pl.when(wanted)

    def peer(offset):
        return layer * SIDE + (place + offset) % SIDE

    def remote(src, dst, send, recv, target):
        return pltpu.make_async_remote_copy(
            src_ref=src,
            dst_ref=dst,
            send_sem=send,
            recv_sem=recv,
            device_id={"ctx": target},
            device_id_type=MESH,
        )

    def stacked(pieces):
        return query_ref.at[pl.ds(0, pieces * unit * HEAD_SIZE // query_ref.shape[1]), :]

    def pack(c):
        kind, g, start, count = parts[c]
        return pltpu.make_async_copy(
            (key_hbm, value_hbm)[kind].at[pl.ds(start, count), pl.ds(g * HEAD_SIZE, HEAD_SIZE)],
            gathered[c].at[0],
            local_sem.at[1],
        )

    def fetch_queries(g):
        columns = pl.ds(g * GROUP_WIDTH * HEAD_SIZE, GROUP_WIDTH * HEAD_SIZE)
        return pltpu.make_async_copy(
            query_hbm.at[:, columns], query_ref.at[:, columns], local_sem.at[2]
        )

    def request(offset):
        slot = request_vmem.at[place]
        return remote(
            slot, slot, request_send, request_recv.at[0], peer(offset)
        )

    def request_down(q):
        return remote(
            request_vmem.at[place],
            request_vmem.at[SIDE + place],
            request_send,
            request_recv.at[1],
            (top - 1) * SIDE + q,
        )

    def wait_bytes(ref, semaphore):
        pltpu.make_async_copy(ref, ref, semaphore).wait()

    def spread(c, offset):
        target = (place + offset) % SIDE
        return remote(
            gathered[c].at[0, quarter_of(c, target), :],
            stores[c].at[me],
            pass_send,
            layer_recv.at[together[c]],
            peer(offset),
        )

    def direct(c, q):
        return remote(
            gathered[c].at[0, quarter_of(c, q), :],
            stores[c].at[me],
            pass_send,
            below_recv.at[c],
            (layer + 1) % LAYERS * SIDE + q,
        )

    def chain(c, source_layer):
        part = stores[c].at[pl.ds(source_layer * SIDE, SIDE)]
        return remote(
            part,
            part,
            pass_send,
            below_recv.at[c],
            (layer + 1) % LAYERS * SIDE + place,
        )

    def deliver(c, offset):
        return remote(
            outgoing[c].at[offset - 1],
            gathered[c].at[pl.ds(1, 2), quarter_of(c, place), :],
            deliver_send,
            deliver_recv.at[together[c]],
            peer(offset),
        )

    def choices_of(q):
        return (1,) if q == SIDE - 1 else (0, 1)

    def deliver_up(c, q):
        span = len(choices_of(q))
        return remote(
            outgoing[c].at[SIDE - 1 + q, pl.ds(2 - span, span)],
            gathered[c].at[pl.ds(3 - span, span), quarter_of(c, place), :],
            pass_send,
            deliver_recv.at[together[c]],
            top * SIDE + q,
        )

    def dense(c, source, target, slot, recv):
        return remote(
            gathered[c].at[source],
            gathered[c].at[3 + slot],
            pass_send,
            recv.at[together[c] if recv is layer_recv else c],
            top * SIDE + target,
        )

    def dense_of(c, q):
        plan = {
            0: ((1, 0, below_recv), (2, 0, layer_recv)),
            1: ((3, 1, layer_recv),),
            2: ((3, 2, below_recv),),
            3: (),
        }[q]
        return [dense(c, 0, *target) for target in plan]

    def relay_of(c, q):
        return dense(c, 3, 3, 0, below_recv) if q == 2 else dense(c, 4, 2, 1, below_recv)

    def on_place(q):
        return pl.when(me == top * SIDE + q)

    fetch_selected = pltpu.make_async_copy(selected_hbm, selected_ref, local_sem.at[0])
    fetch_selected.start()
    for c in range(chunks):
        pack(c).start()
    for g in range(heads):
        fetch_queries(g).start()

    barrier = pltpu.get_barrier_semaphore()
    for offset in range(1, SIDE):
        pl.semaphore_signal(barrier, inc=1, device_id={"ctx": peer(offset)}, device_id_type=MESH)

    @pl.when(layer > 0)
    def _():
        for q in range(SIDE):
            pl.semaphore_signal(
                barrier, inc=1, device_id={"ctx": (layer - 1) * SIDE + q}, device_id_type=MESH
            )

    @pl.when(layer < top)
    def _():
        for q in range(SIDE):
            pl.semaphore_signal(
                barrier, inc=1, device_id={"ctx": (layer + 1) * SIDE + q}, device_id_type=MESH
            )

    neighbour_layers = jnp.minimum(layer, 1) + jnp.minimum(top - layer, 1)
    pl.semaphore_wait(barrier, SIDE - 1 + SIDE * neighbour_layers)

    wait_bytes(stacked(2 * heads * SIDE), local_sem.at[1])

    @on_layer(0, 1)
    def _():
        for c in range(AHEAD):
            for q in range(SIDE):
                direct(c, q).start()

    @on_layer(0)
    def _():
        for c in range(AHEAD, DIRECT):
            for q in range(SIDE):
                direct(c, q).start()

    fetch_selected.wait()
    lane = lax.broadcasted_iota(jnp.int32, (1, 128), 1)
    request_vmem[place] = jnp.where(lane == 0, selected_ref[0, 0], selected_ref[0, 1])

    @on_layer(top)
    def _():
        for q in range(SIDE):
            request_down(q).start()

    @pl.when(layer < top)
    def _():
        for offset in range(1, SIDE):
            request(offset).start()

    for c in range(chunks):
        @pl.when(layer < top)
        def _():
            for offset in range(1, SIDE):
                spread(c, offset).start()
            stores[c][me] = gathered[c][0, quarter_of(c, place), :]

        for q in range(SIDE - 1):

            @on_place(q)
            def _():
                for copy in dense_of(c, q):
                    copy.start()

    first_valid = selected_ref[0, 0] < me
    second_valid = jnp.logical_and(
        selected_ref[0, 1] < me, selected_ref[0, 1] != selected_ref[0, 0]
    )
    causal = causal_mask(rows)

    def slot_of(choice):
        wanted = selected_ref[0, choice]
        local = jnp.logical_and(layer == top, wanted >= top * SIDE)
        return jnp.where(local, 3 + wanted - top * SIDE, 1 + choice)

    def rows_from(c, slot):
        return gathered[c][slot_of(slot - 1) if slot else 0]

    def wait_pieces(c, pieces, semaphore):
        wait_bytes(stores[c].at[pl.ds(0, pieces)], semaphore.at[c])

    def wait_group(c, pieces, semaphore):
        k = together[c]
        if c == sum(GROUPS[:k]):
            size = GROUPS[k] * pieces * parts[c][3] // SIDE * 2 * HEAD_SIZE
            wait_bytes(total_ref.at[0, pl.ds(0, size // (8 * HEAD_SIZE))], semaphore.at[k])

    @on_layer(1)
    def _():
        for c in range(AHEAD):
            wait_pieces(c, SIDE, below_recv)
            chain(c, 0).start()
        for c in range(AHEAD, DIRECT):
            for q in range(SIDE):
                direct(c, q).start()

    @pl.when(layer < top)
    def _():
        wait_bytes(request_vmem.at[pl.ds(0, SIDE - 1)], request_recv.at[0])

    @on_layer(top - 1)
    def _():
        wait_bytes(request_vmem.at[pl.ds(0, SIDE)], request_recv.at[1])

    @pl.when(layer != top - 1)
    def _():
        for q in range(SIDE):
            request_vmem[SIDE + q] = jnp.zeros((1, 128), jnp.int32)

    @on_layer(top)
    def _():
        for offset in range(1, SIDE):
            request_vmem[(place + offset) % SIDE] = jnp.zeros((1, 128), jnp.int32)

    to_smem = pltpu.make_async_copy(request_vmem, request_smem, local_sem.at[0])
    to_smem.start()
    to_smem.wait()

    def hand_out(c):
        for offset in range(1, SIDE):
            for choice in range(2):
                wanted = request_smem[(place + offset) % SIDE, 0, choice]
                outgoing[c][offset - 1, choice] = stores[c][wanted]
            deliver(c, offset).start()
        for choice in range(2):
            gathered[c][1 + choice, quarter_of(c, place), :] = stores[c][request_smem[place, 0, choice]]

    def hand_up(c):
        for q in range(SIDE):
            for choice in choices_of(q):
                wanted = jnp.minimum(request_smem[SIDE + q, 0, choice], top * SIDE - 1)
                outgoing[c][SIDE - 1 + q, choice] = stores[c][wanted]
            deliver_up(c, q).start()

    def serve_bottom(c):
        wait_group(c, SIDE - 1, layer_recv)
        if c >= DIRECT:
            chain(c, 0).start()
        hand_out(c)

    def serve_second(c):
        if c >= AHEAD:
            wait_pieces(c, SIDE, below_recv)
            chain(c, 0).start()
        if c == 0:
            for early in range(DIRECT):
                wait_group(early, SIDE - 1, layer_recv)
        if DIRECT <= c + 1 < chunks:
            wait_group(c + 1, SIDE - 1, layer_recv)
            chain(c + 1, 1).start()
        hand_out(c)

    def serve_third(c):
        wait_group(c, SIDE - 1, layer_recv)
        wait_pieces(c, 2 * SIDE, below_recv)
        hand_up(c)
        hand_out(c)

    def serve_top(c):
        @pl.when(place >= 2)
        def _():
            wait_group(c, SIDE, layer_recv)

        for q in (2, 3):

            @on_place(q)
            def _():
                relay_of(c, q).start()

    def serve(step):
        works = (serve_bottom, serve_second, serve_third, serve_top)
        for number, (work, plan) in enumerate(zip(works, SERVED)):
            if plan[step] < plan[step + 1]:

                @on_layer(number)
                def _():
                    for c in range(plan[step], plan[step + 1]):
                        work(c)

    def wait_delivery(c):
        @pl.when(layer < top)
        def _():
            wait_group(c, 2 * (SIDE - 1), deliver_recv)

        for q in range(SIDE):

            @on_place(q)
            def _():
                wait_group(c, SIDE * len(choices_of(q)), deliver_recv)
                if q > 0:
                    wait_pieces(c, SIDE * (2 if q == 3 else 1), below_recv)

    def head_columns(g, index):
        return pl.ds((g * GROUP_WIDTH + index) * HEAD_SIZE, HEAD_SIZE)

    def weigh_group(run, heads_of=range(GROUP_WIDTH)):
        if heads_of[0] == 0:
            for c in run:
                wait_delivery(c)
        g = parts[run[0]][1]
        keys = jnp.concatenate([rows_from(c, slot) for slot in range(3) for c in run], axis=0)
        for index in heads_of:
            weight_ref[g % 2 * GROUP_WIDTH + index] = weigh(
                query_ref[:, head_columns(g, index)], keys, causal, first_valid, second_valid
            )

    def mix_group(arriving, runs, begins=True, ends=True):
        for c in arriving:
            wait_delivery(c)
        g = parts[arriving[0]][1]
        values = with_ones(
            jnp.concatenate([rows_from(c, slot) for slot, run in runs for c in run], axis=0)
        )
        for index in range(GROUP_WIDTH):
            weights = jnp.concatenate(
                [
                    weight_ref[
                        g % 2 * GROUP_WIDTH + index,
                        :,
                        pl.ds(slot * rows + parts[run[0]][2], sum(parts[c][3] for c in run)),
                    ]
                    for slot, run in runs
                ],
                axis=1,
            )
            mixture = jnp.dot(weights, values, preferred_element_type=jnp.float32)
            if not begins:
                mixture += total_ref[index]
            if ends:
                out_ref[:, head_columns(g, index)] = normalised(mixture)
            else:
                total_ref[index] = mixture

    def mix_whole(*run):
        mix_group(run, [(slot, run) for slot in range(3)])

    low, high = range(GROUP_WIDTH // 2), range(GROUP_WIDTH // 2, GROUP_WIDTH)
    serve(0)
    wait_bytes(query_ref, local_sem.at[2])
    weigh_group((0, 1))
    serve(1)
    mix_whole(2, 3)
    serve(2)
    weigh_group((4, 5))
    serve(3)
    mix_whole(6, 7)
    serve(4)
    weigh_group((8, 9), low)
    serve(5)
    weigh_group((8, 9), high)
    serve(6)
    weigh_group((10, 11), low)
    serve(7)
    weigh_group((10, 11), high)
    serve(8)
    mix_whole(12, 13, 14, 15)
    mix_group((16, 17), [(0, (16, 17, 18, 19)), (1, (16, 17)), (2, (16, 17))], ends=False)
    mix_group((18, 19), [(1, (18, 19)), (2, (18, 19))], begins=False)

    full = 2 * heads
    within = full * (SIDE - 1)
    passed = (
        within + full * SIDE,
        within + full * SIDE + full * SIDE,
        within + full * (2 * SIDE - 1),
    )
    for number, pieces in enumerate(passed):

        @on_layer(number)
        def _():
            wait_bytes(stacked(pieces), pass_send)
            wait_bytes(weight_ref.at[pl.ds(0, 2)], deliver_send)
            wait_bytes(request_vmem.at[pl.ds(0, SIDE - 1)], request_send)

    @on_layer(top)
    def _():
        wait_bytes(request_vmem.at[pl.ds(0, SIDE)], request_send)

    for q, blocks in enumerate((2, 1, 2, 1)):

        @on_place(q)
        def _():
            wait_bytes(stacked(full * blocks * SIDE), pass_send)


def relayed(queries, all_key_states, all_value_states, selected):
    rows = queries.shape[0]
    counts = [count for _, _, _, count in parts_of(rows)]
    chunks = len(counts)
    blocks = LAYERS * SIDE
    kind = all_key_states.dtype
    dma = pltpu.SemaphoreType.DMA
    return pl.pallas_call(
        functools.partial(relay_kernel, rows),
        out_shape=pltpu.VMEM(queries.shape, queries.dtype),
        in_specs=[pl.BlockSpec(memory_space=pltpu.HBM)] * 4,
        out_specs=pl.BlockSpec(memory_space=pltpu.VMEM),
        scratch_shapes=[pltpu.VMEM((blocks, n // SIDE, HEAD_SIZE), kind) for n in counts]
        + [pltpu.VMEM((2 * SIDE - 1, 2, n // SIDE, HEAD_SIZE), kind) for n in counts]
        + [pltpu.VMEM((6, n, HEAD_SIZE), kind) for n in counts]
        + [
            pltpu.VMEM(queries.shape, queries.dtype),
            pltpu.VMEM((2 * GROUP_WIDTH, rows, 3 * rows), kind),
            pltpu.VMEM((GROUP_WIDTH, rows, 2 * HEAD_SIZE), jnp.float32),
            pltpu.VMEM((2 * SIDE, 1, 128), jnp.int32),
            pltpu.SMEM((2 * SIDE, 1, 128), jnp.int32),
            pltpu.SMEM((1, 2), jnp.int32),
            dma((3,)),
            dma,
            dma((2,)),
            dma((len(GROUPS),)),
            dma((chunks,)),
            dma((len(GROUPS),)),
            dma,
            dma,
        ],
        compiler_params=pltpu.CompilerParams(
            collective_id=0, has_side_effects=True, vmem_limit_bytes=123 * 2**19
        ),
    )(selected, queries, all_key_states, all_value_states)


def attend_kernel(valid_ref, query_ref, key_ref, value_ref, out_ref):
    rows = query_ref.shape[0]
    causal = lax.broadcasted_iota(jnp.int32, (rows, rows), 1) <= lax.broadcasted_iota(
        jnp.int32, (rows, rows), 0
    )
    out_ref[...] = attend_head(
        query_ref[...],
        key_ref[...],
        with_ones(value_ref[...]),
        causal,
        valid_ref[0] != 0,
        valid_ref[1] != 0,
    )


def exchanged(queries, all_key_states, all_value_states, selected):
    devices = lax.axis_size("ctx")
    me = lax.axis_index("ctx")
    rows, width = all_key_states.shape
    exchange = functools.partial(
        lax.all_to_all, axis_name="ctx", split_axis=0, concat_axis=0, tiled=True
    )
    both = jnp.concatenate([all_key_states, all_value_states], axis=1)
    requests = lax.all_gather(selected, "ctx", axis=0, tiled=True)
    held = exchange(both.reshape(devices, rows // devices, 2 * width))
    flat = held.reshape(devices, rows // devices * 2 * width)
    numbers = jnp.arange(devices, dtype=requests.dtype)

    def picked(choice):
        pick = (requests[:, choice, None] == numbers[None, :]).astype(flat.dtype)
        taken = jnp.dot(pick, flat, preferred_element_type=jnp.float32).astype(flat.dtype)
        return exchange(taken.reshape(held.shape)).reshape(rows, 2 * width)

    chosen = [picked(choice) for choice in range(2)]
    everything = jnp.concatenate([both] + chosen, axis=0)
    first, second = selected[0, 0], selected[0, 1]
    valid = jnp.stack([first < me, jnp.logical_and(second < me, second != first)])
    return pl.pallas_call(
        attend_kernel,
        out_shape=jax.ShapeDtypeStruct(queries.shape, queries.dtype),
        grid=(QUERY_HEADS,),
        in_specs=[
            pl.BlockSpec(memory_space=pltpu.SMEM),
            pl.BlockSpec((rows, HEAD_SIZE), lambda h: (0, h)),
            pl.BlockSpec((3 * rows, HEAD_SIZE), lambda h: (0, h // GROUP_WIDTH)),
            pl.BlockSpec((3 * rows, HEAD_SIZE), lambda h: (0, KEY_VALUE_HEADS + h // GROUP_WIDTH)),
        ],
        out_specs=pl.BlockSpec((rows, HEAD_SIZE), lambda h: (0, h)),
    )(valid.astype(jnp.int32), queries, everything, everything)


def solution(mesh):
    placed = P(("groups", "ctx"), None)
    local = relayed if mesh.shape["ctx"] == LAYERS * SIDE else exchanged
    return jax.shard_map(
        local, mesh=mesh, in_specs=(placed,) * 4, out_specs=placed, check_vma=False
    )
```

```python
import functools
import math

import jax
import jax.numpy as jnp
from jax import lax
from jax.experimental import pallas as pl
from jax.experimental.pallas import tpu as pltpu
from jax.sharding import PartitionSpec as P

QUERY_HEADS = 32
KEY_VALUE_HEADS = 4
HEAD_SIZE = 128
GROUP_WIDTH = QUERY_HEADS // KEY_VALUE_HEADS
EXPONENT_SCALE = math.log2(math.e) / math.sqrt(HEAD_SIZE)
MASKED = -1e30
LAYERS = 4
SIDE = 4
DIRECT = 6
AHEAD = 4
SERVED = (
    (0, 20, 20, 20, 20, 20, 20, 20, 20, 20),
    (0, 10, 12, 16, 20, 20, 20, 20, 20, 20),
    (0, 7, 8, 9, 11, 13, 15, 17, 20, 20),
    (0, 6, 8, 12, 20, 20, 20, 20, 20, 20),
)
GROUPS = (2, 2, 2, 2, 2, 2, 4, 2, 2)
MESH = pl.DeviceIdType.MESH


def half_max(scores):
    return jnp.maximum(scores[:, :HEAD_SIZE], scores[:, HEAD_SIZE:])


def weigh(queries, keys, causal, first_valid, second_valid):
    rows = queries.shape[0]
    scores = lax.dot_general(
        queries, keys, (((1,), (1,)), ((), ())), preferred_element_type=jnp.float32
    )
    own = jnp.where(causal, scores[:, :rows], MASKED)
    first = scores[:, rows : 2 * rows]
    second = scores[:, 2 * rows :]
    row_max = jnp.max(
        jnp.maximum(
            half_max(own),
            jnp.maximum(
                jnp.where(first_valid, half_max(first), MASKED),
                jnp.where(second_valid, half_max(second), MASKED),
            ),
        ),
        axis=1,
        keepdims=True,
    )
    first_max = jnp.where(first_valid, row_max, -MASKED)
    second_max = jnp.where(second_valid, row_max, -MASKED)
    return jnp.concatenate(
        [
            jnp.exp2((part - top) * EXPONENT_SCALE).astype(jnp.bfloat16)
            for part, top in ((own, row_max), (first, first_max), (second, second_max))
        ],
        axis=1,
    )


def normalised(mixture):
    return (mixture[:, :HEAD_SIZE] * (1.0 / mixture[:, HEAD_SIZE:])).astype(jnp.bfloat16)


def mix(weights, values):
    return normalised(jnp.dot(weights, values, preferred_element_type=jnp.float32))


def attend_head(queries, keys, values, causal, first_valid, second_valid):
    return mix(weigh(queries, keys, causal, first_valid, second_valid), values)


def with_ones(values):
    return jnp.concatenate([values, jnp.ones_like(values)], axis=1)


def causal_mask(rows):
    return lax.broadcasted_iota(jnp.int32, (rows, rows), 1) <= lax.broadcasted_iota(
        jnp.int32, (rows, rows), 0
    )


def parts_of(rows):
    order = ((0, 0, 2), (1, 0, 2), (0, 1, 2), (1, 1, 2), (0, 2, 2), (0, 3, 2), (1, 2, 4), (1, 3, 4))
    return [
        (kind, g, rows // cuts * i, rows // cuts) for kind, g, cuts in order for i in range(cuts)
    ]


def relay_kernel(rows, selected_hbm, query_hbm, key_hbm, value_hbm, out_ref, *scratch):
    heads = KEY_VALUE_HEADS
    parts = parts_of(rows)
    chunks = len(parts)
    together = [k for k, count in enumerate(GROUPS) for _ in range(count)]
    stores = scratch[:chunks]
    outgoing = scratch[chunks : 2 * chunks]
    gathered = scratch[2 * chunks : 3 * chunks]
    (
        query_ref,
        weight_ref,
        total_ref,
        request_vmem,
        request_smem,
        selected_ref,
        local_sem,
        request_send,
        request_recv,
        layer_recv,
        below_recv,
        deliver_recv,
        pass_send,
        deliver_send,
    ) = scratch[3 * chunks :]
    unit = rows // SIDE
    top = LAYERS - 1
    me = lax.axis_index("ctx")
    layer = me // SIDE
    place = me % SIDE

    def quarter_of(c, q):
        size = parts[c][3] // SIDE
        return pl.ds(q * size, size)

    def on_layer(*layers):
        wanted = layer == layers[0]
        for other in layers[1:]:
            wanted = jnp.logical_or(wanted, layer == other)
        return pl.when(wanted)

    def peer(offset):
        return layer * SIDE + (place + offset) % SIDE

    def remote(src, dst, send, recv, target):
        return pltpu.make_async_remote_copy(
            src_ref=src,
            dst_ref=dst,
            send_sem=send,
            recv_sem=recv,
            device_id={"ctx": target},
            device_id_type=MESH,
        )

    def stacked(pieces):
        return query_ref.at[pl.ds(0, pieces * unit * HEAD_SIZE // query_ref.shape[1]), :]

    def pack(c):
        kind, g, start, count = parts[c]
        return pltpu.make_async_copy(
            (key_hbm, value_hbm)[kind].at[pl.ds(start, count), pl.ds(g * HEAD_SIZE, HEAD_SIZE)],
            gathered[c].at[0],
            local_sem.at[1],
        )

    def fetch_queries(g):
        columns = pl.ds(g * GROUP_WIDTH * HEAD_SIZE, GROUP_WIDTH * HEAD_SIZE)
        return pltpu.make_async_copy(
            query_hbm.at[:, columns], query_ref.at[:, columns], local_sem.at[2]
        )

    def request(offset):
        slot = request_vmem.at[place]
        return remote(
            slot, slot, request_send, request_recv.at[0], peer(offset)
        )

    def request_down(q):
        return remote(
            request_vmem.at[place],
            request_vmem.at[SIDE + place],
            request_send,
            request_recv.at[1],
            (top - 1) * SIDE + q,
        )

    def wait_bytes(ref, semaphore):
        pltpu.make_async_copy(ref, ref, semaphore).wait()

    def spread(c, offset):
        target = (place + offset) % SIDE
        return remote(
            gathered[c].at[0, quarter_of(c, target), :],
            stores[c].at[me],
            pass_send,
            layer_recv.at[together[c]],
            peer(offset),
        )

    def direct(c, q):
        return remote(
            gathered[c].at[0, quarter_of(c, q), :],
            stores[c].at[me],
            pass_send,
            below_recv.at[c],
            (layer + 1) % LAYERS * SIDE + q,
        )

    def chain(c, source_layer):
        part = stores[c].at[pl.ds(source_layer * SIDE, SIDE)]
        return remote(
            part,
            part,
            pass_send,
            below_recv.at[c],
            (layer + 1) % LAYERS * SIDE + place,
        )

    def deliver(c, offset):
        return remote(
            outgoing[c].at[offset - 1],
            gathered[c].at[pl.ds(1, 2), quarter_of(c, place), :],
            deliver_send,
            deliver_recv.at[together[c]],
            peer(offset),
        )

    def choices_of(q):
        return (1,) if q == SIDE - 1 else (0, 1)

    def deliver_up(c, q):
        span = len(choices_of(q))
        return remote(
            outgoing[c].at[SIDE - 1 + q, pl.ds(2 - span, span)],
            gathered[c].at[pl.ds(3 - span, span), quarter_of(c, place), :],
            pass_send,
            deliver_recv.at[together[c]],
            top * SIDE + q,
        )

    def dense(c, source, target, slot, recv):
        return remote(
            gathered[c].at[source],
            gathered[c].at[3 + slot],
            pass_send,
            recv.at[together[c] if recv is layer_recv else c],
            top * SIDE + target,
        )

    def dense_of(c, q):
        plan = {
            0: ((1, 0, below_recv), (2, 0, layer_recv)),
            1: ((3, 1, layer_recv),),
            2: ((3, 2, below_recv),),
            3: (),
        }[q]
        return [dense(c, 0, *target) for target in plan]

    def relay_of(c, q):
        return dense(c, 3, 3, 0, below_recv) if q == 2 else dense(c, 4, 2, 1, below_recv)

    def on_place(q):
        return pl.when(me == top * SIDE + q)

    fetch_selected = pltpu.make_async_copy(selected_hbm, selected_ref, local_sem.at[0])
    fetch_selected.start()
    for c in range(chunks):
        pack(c).start()
    for g in range(heads):
        fetch_queries(g).start()

    barrier = pltpu.get_barrier_semaphore()
    for offset in range(1, SIDE):
        pl.semaphore_signal(barrier, inc=1, device_id={"ctx": peer(offset)}, device_id_type=MESH)

    @pl.when(layer > 0)
    def _():
        for q in range(SIDE):
            pl.semaphore_signal(
                barrier, inc=1, device_id={"ctx": (layer - 1) * SIDE + q}, device_id_type=MESH
            )

    @pl.when(layer < top)
    def _():
        for q in range(SIDE):
            pl.semaphore_signal(
                barrier, inc=1, device_id={"ctx": (layer + 1) * SIDE + q}, device_id_type=MESH
            )

    neighbour_layers = jnp.minimum(layer, 1) + jnp.minimum(top - layer, 1)
    pl.semaphore_wait(barrier, SIDE - 1 + SIDE * neighbour_layers)

    wait_bytes(stacked(2 * heads * SIDE), local_sem.at[1])

    @on_layer(0, 1)
    def _():
        for c in range(AHEAD):
            for q in range(SIDE):
                direct(c, q).start()

    late = jnp.logical_and(layer == 1, place >= SIDE // 2)

    @pl.when(jnp.logical_or(layer == 0, late))
    def _():
        for q in range(SIDE):
            direct(AHEAD, q).start()

    @on_layer(0)
    def _():
        for c in range(AHEAD + 1, DIRECT):
            for q in range(SIDE):
                direct(c, q).start()

    fetch_selected.wait()
    lane = lax.broadcasted_iota(jnp.int32, (1, 128), 1)
    request_vmem[place] = jnp.where(lane == 0, selected_ref[0, 0], selected_ref[0, 1])

    @on_layer(top)
    def _():
        for q in range(SIDE):
            request_down(q).start()

    @pl.when(layer < top)
    def _():
        for offset in range(1, SIDE):
            request(offset).start()

    for c in range(chunks):
        @pl.when(layer < top)
        def _():
            for offset in range(1, SIDE):
                spread(c, offset).start()
            stores[c][me] = gathered[c][0, quarter_of(c, place), :]

        for q in range(SIDE - 1):

            @on_place(q)
            def _():
                for copy in dense_of(c, q):
                    copy.start()

    first_valid = selected_ref[0, 0] < me
    second_valid = jnp.logical_and(
        selected_ref[0, 1] < me, selected_ref[0, 1] != selected_ref[0, 0]
    )
    causal = causal_mask(rows)

    def slot_of(choice):
        wanted = selected_ref[0, choice]
        local = jnp.logical_and(layer == top, wanted >= top * SIDE)
        return jnp.where(local, 3 + wanted - top * SIDE, 1 + choice)

    def rows_from(c, slot):
        return gathered[c][slot_of(slot - 1) if slot else 0]

    def wait_pieces(c, pieces, semaphore):
        wait_bytes(stores[c].at[pl.ds(0, pieces)], semaphore.at[c])

    def wait_group(c, pieces, semaphore):
        k = together[c]
        if c == sum(GROUPS[:k]):
            size = GROUPS[k] * pieces * parts[c][3] // SIDE * 2 * HEAD_SIZE
            wait_bytes(total_ref.at[0, pl.ds(0, size // (8 * HEAD_SIZE))], semaphore.at[k])

    @on_layer(1)
    def _():
        for c in range(AHEAD):
            wait_pieces(c, SIDE, below_recv)
            chain(c, 0).start()

        @pl.when(place < SIDE // 2)
        def _():
            for q in range(SIDE):
                direct(AHEAD, q).start()

        for c in range(AHEAD + 1, DIRECT):
            for q in range(SIDE):
                direct(c, q).start()

    @pl.when(layer < top)
    def _():
        wait_bytes(request_vmem.at[pl.ds(0, SIDE - 1)], request_recv.at[0])

    @on_layer(top - 1)
    def _():
        wait_bytes(request_vmem.at[pl.ds(0, SIDE)], request_recv.at[1])

    @pl.when(layer != top - 1)
    def _():
        for q in range(SIDE):
            request_vmem[SIDE + q] = jnp.zeros((1, 128), jnp.int32)

    @on_layer(top)
    def _():
        for offset in range(1, SIDE):
            request_vmem[(place + offset) % SIDE] = jnp.zeros((1, 128), jnp.int32)

    to_smem = pltpu.make_async_copy(request_vmem, request_smem, local_sem.at[0])
    to_smem.start()
    to_smem.wait()

    def hand_out(c):
        for offset in range(1, SIDE):
            for choice in range(2):
                wanted = request_smem[(place + offset) % SIDE, 0, choice]
                outgoing[c][offset - 1, choice] = stores[c][wanted]
            deliver(c, offset).start()
        for choice in range(2):
            gathered[c][1 + choice, quarter_of(c, place), :] = stores[c][request_smem[place, 0, choice]]

    def hand_up(c):
        for q in range(SIDE):
            for choice in choices_of(q):
                wanted = jnp.minimum(request_smem[SIDE + q, 0, choice], top * SIDE - 1)
                outgoing[c][SIDE - 1 + q, choice] = stores[c][wanted]
            deliver_up(c, q).start()

    def serve_bottom(c):
        wait_group(c, SIDE - 1, layer_recv)
        if c >= DIRECT:
            chain(c, 0).start()
        hand_out(c)

    def serve_second(c):
        if c >= AHEAD:
            wait_pieces(c, SIDE, below_recv)
            chain(c, 0).start()
        if c == 0:
            for early in range(DIRECT):
                wait_group(early, SIDE - 1, layer_recv)
        if DIRECT <= c + 1 < chunks:
            wait_group(c + 1, SIDE - 1, layer_recv)
            chain(c + 1, 1).start()
        hand_out(c)

    def serve_third(c):
        wait_group(c, SIDE - 1, layer_recv)
        wait_pieces(c, 2 * SIDE, below_recv)
        hand_up(c)
        hand_out(c)

    def serve_top(c):
        @pl.when(place >= 2)
        def _():
            wait_group(c, SIDE, layer_recv)

        for q in (2, 3):

            @on_place(q)
            def _():
                relay_of(c, q).start()

    def serve(step):
        works = (serve_bottom, serve_second, serve_third, serve_top)
        for number, (work, plan) in enumerate(zip(works, SERVED)):
            if plan[step] < plan[step + 1]:

                @on_layer(number)
                def _():
                    for c in range(plan[step], plan[step + 1]):
                        work(c)

    def wait_delivery(c):
        @pl.when(layer < top)
        def _():
            wait_group(c, 2 * (SIDE - 1), deliver_recv)

        for q in range(SIDE):

            @on_place(q)
            def _():
                wait_group(c, SIDE * len(choices_of(q)), deliver_recv)
                if q > 0:
                    wait_pieces(c, SIDE * (2 if q == 3 else 1), below_recv)

    def head_columns(g, index):
        return pl.ds((g * GROUP_WIDTH + index) * HEAD_SIZE, HEAD_SIZE)

    def weigh_group(run, heads_of=range(GROUP_WIDTH)):
        if heads_of[0] == 0:
            for c in run:
                wait_delivery(c)
        g = parts[run[0]][1]
        keys = jnp.concatenate([rows_from(c, slot) for slot in range(3) for c in run], axis=0)
        for index in heads_of:
            weight_ref[g % 2 * GROUP_WIDTH + index] = weigh(
                query_ref[:, head_columns(g, index)], keys, causal, first_valid, second_valid
            )

    def mix_group(arriving, runs, begins=True, ends=True):
        for c in arriving:
            wait_delivery(c)
        g = parts[arriving[0]][1]
        values = with_ones(
            jnp.concatenate([rows_from(c, slot) for slot, run in runs for c in run], axis=0)
        )
        for index in range(GROUP_WIDTH):
            weights = jnp.concatenate(
                [
                    weight_ref[
                        g % 2 * GROUP_WIDTH + index,
                        :,
                        pl.ds(slot * rows + parts[run[0]][2], sum(parts[c][3] for c in run)),
                    ]
                    for slot, run in runs
                ],
                axis=1,
            )
            mixture = jnp.dot(weights, values, preferred_element_type=jnp.float32)
            if not begins:
                mixture += total_ref[index]
            if ends:
                out_ref[:, head_columns(g, index)] = normalised(mixture)
            else:
                total_ref[index] = mixture

    def mix_whole(*run):
        mix_group(run, [(slot, run) for slot in range(3)])

    low, high = range(GROUP_WIDTH // 2), range(GROUP_WIDTH // 2, GROUP_WIDTH)
    serve(0)
    wait_bytes(query_ref, local_sem.at[2])
    weigh_group((0, 1))
    serve(1)
    mix_whole(2, 3)
    serve(2)
    weigh_group((4, 5))
    serve(3)
    mix_whole(6, 7)
    serve(4)
    weigh_group((8, 9), low)
    serve(5)
    weigh_group((8, 9), high)
    serve(6)
    weigh_group((10, 11), low)
    serve(7)
    weigh_group((10, 11), high)
    serve(8)
    mix_whole(12, 13, 14, 15)
    mix_group((16, 17), [(0, (16, 17, 18, 19)), (1, (16, 17)), (2, (16, 17))], ends=False)
    mix_group((18, 19), [(1, (18, 19)), (2, (18, 19))], begins=False)

    full = 2 * heads
    within = full * (SIDE - 1)
    passed = (
        within + full * SIDE,
        within + full * SIDE + full * SIDE,
        within + full * (2 * SIDE - 1),
    )
    for number, pieces in enumerate(passed):

        @on_layer(number)
        def _():
            wait_bytes(stacked(pieces), pass_send)
            wait_bytes(weight_ref.at[pl.ds(0, 2)], deliver_send)
            wait_bytes(request_vmem.at[pl.ds(0, SIDE - 1)], request_send)

    @on_layer(top)
    def _():
        wait_bytes(request_vmem.at[pl.ds(0, SIDE)], request_send)

    for q, blocks in enumerate((2, 1, 2, 1)):

        @on_place(q)
        def _():
            wait_bytes(stacked(full * blocks * SIDE), pass_send)


def relayed(queries, all_key_states, all_value_states, selected):
    rows = queries.shape[0]
    counts = [count for _, _, _, count in parts_of(rows)]
    chunks = len(counts)
    blocks = LAYERS * SIDE
    kind = all_key_states.dtype
    dma = pltpu.SemaphoreType.DMA
    return pl.pallas_call(
        functools.partial(relay_kernel, rows),
        out_shape=pltpu.VMEM(queries.shape, queries.dtype),
        in_specs=[pl.BlockSpec(memory_space=pltpu.HBM)] * 4,
        out_specs=pl.BlockSpec(memory_space=pltpu.VMEM),
        scratch_shapes=[pltpu.VMEM((blocks, n // SIDE, HEAD_SIZE), kind) for n in counts]
        + [pltpu.VMEM((2 * SIDE - 1, 2, n // SIDE, HEAD_SIZE), kind) for n in counts]
        + [pltpu.VMEM((6, n, HEAD_SIZE), kind) for n in counts]
        + [
            pltpu.VMEM(queries.shape, queries.dtype),
            pltpu.VMEM((2 * GROUP_WIDTH, rows, 3 * rows), kind),
            pltpu.VMEM((GROUP_WIDTH, rows, 2 * HEAD_SIZE), jnp.float32),
            pltpu.VMEM((2 * SIDE, 1, 128), jnp.int32),
            pltpu.SMEM((2 * SIDE, 1, 128), jnp.int32),
            pltpu.SMEM((1, 2), jnp.int32),
            dma((3,)),
            dma,
            dma((2,)),
            dma((len(GROUPS),)),
            dma((chunks,)),
            dma((len(GROUPS),)),
            dma,
            dma,
        ],
        compiler_params=pltpu.CompilerParams(
            collective_id=0, has_side_effects=True, vmem_limit_bytes=123 * 2**19
        ),
    )(selected, queries, all_key_states, all_value_states)


def attend_kernel(valid_ref, query_ref, key_ref, value_ref, out_ref):
    rows = query_ref.shape[0]
    causal = lax.broadcasted_iota(jnp.int32, (rows, rows), 1) <= lax.broadcasted_iota(
        jnp.int32, (rows, rows), 0
    )
    out_ref[...] = attend_head(
        query_ref[...],
        key_ref[...],
        with_ones(value_ref[...]),
        causal,
        valid_ref[0] != 0,
        valid_ref[1] != 0,
    )


def exchanged(queries, all_key_states, all_value_states, selected):
    devices = lax.axis_size("ctx")
    me = lax.axis_index("ctx")
    rows, width = all_key_states.shape
    exchange = functools.partial(
        lax.all_to_all, axis_name="ctx", split_axis=0, concat_axis=0, tiled=True
    )
    both = jnp.concatenate([all_key_states, all_value_states], axis=1)
    requests = lax.all_gather(selected, "ctx", axis=0, tiled=True)
    held = exchange(both.reshape(devices, rows // devices, 2 * width))
    flat = held.reshape(devices, rows // devices * 2 * width)
    numbers = jnp.arange(devices, dtype=requests.dtype)

    def picked(choice):
        pick = (requests[:, choice, None] == numbers[None, :]).astype(flat.dtype)
        taken = jnp.dot(pick, flat, preferred_element_type=jnp.float32).astype(flat.dtype)
        return exchange(taken.reshape(held.shape)).reshape(rows, 2 * width)

    chosen = [picked(choice) for choice in range(2)]
    everything = jnp.concatenate([both] + chosen, axis=0)
    first, second = selected[0, 0], selected[0, 1]
    valid = jnp.stack([first < me, jnp.logical_and(second < me, second != first)])
    return pl.pallas_call(
        attend_kernel,
        out_shape=jax.ShapeDtypeStruct(queries.shape, queries.dtype),
        grid=(QUERY_HEADS,),
        in_specs=[
            pl.BlockSpec(memory_space=pltpu.SMEM),
            pl.BlockSpec((rows, HEAD_SIZE), lambda h: (0, h)),
            pl.BlockSpec((3 * rows, HEAD_SIZE), lambda h: (0, h // GROUP_WIDTH)),
            pl.BlockSpec((3 * rows, HEAD_SIZE), lambda h: (0, KEY_VALUE_HEADS + h // GROUP_WIDTH)),
        ],
        out_specs=pl.BlockSpec((rows, HEAD_SIZE), lambda h: (0, h)),
    )(valid.astype(jnp.int32), queries, everything, everything)


def solution(mesh):
    placed = P(("groups", "ctx"), None)
    local = relayed if mesh.shape["ctx"] == LAYERS * SIDE else exchanged
    return jax.shard_map(
        local, mesh=mesh, in_specs=(placed,) * 4, out_specs=placed, check_vma=False
    )
```

```python
import functools
import math

import jax
import jax.numpy as jnp
from jax import lax
from jax.experimental import pallas as pl
from jax.experimental.pallas import tpu as pltpu
from jax.sharding import PartitionSpec as P

QUERY_HEADS = 32
KEY_VALUE_HEADS = 4
HEAD_SIZE = 128
GROUP_WIDTH = QUERY_HEADS // KEY_VALUE_HEADS
EXPONENT_SCALE = math.log2(math.e) / math.sqrt(HEAD_SIZE)
MASKED = -1e30
LAYERS = 4
SIDE = 4
DIRECT = 6
AHEAD = 4
SERVED = (
    (0, 20, 20, 20, 20, 20, 20, 20, 20, 20),
    (0, 10, 12, 16, 20, 20, 20, 20, 20, 20),
    (0, 7, 8, 9, 11, 13, 15, 17, 20, 20),
    (0, 6, 8, 12, 20, 20, 20, 20, 20, 20),
)
GROUPS = (2, 2, 2, 2, 2, 2, 4, 2, 2)
MESH = pl.DeviceIdType.MESH


def half_max(scores):
    return jnp.maximum(scores[:, :HEAD_SIZE], scores[:, HEAD_SIZE:])


def weigh(queries, keys, causal, first_valid, second_valid):
    rows = queries.shape[0]
    scores = lax.dot_general(
        queries, keys, (((1,), (1,)), ((), ())), preferred_element_type=jnp.float32
    )
    own = jnp.where(causal, scores[:, :rows], MASKED)
    first = scores[:, rows : 2 * rows]
    second = scores[:, 2 * rows :]
    row_max = jnp.max(
        jnp.maximum(
            half_max(own),
            jnp.maximum(
                jnp.where(first_valid, half_max(first), MASKED),
                jnp.where(second_valid, half_max(second), MASKED),
            ),
        ),
        axis=1,
        keepdims=True,
    )
    first_max = jnp.where(first_valid, row_max, -MASKED)
    second_max = jnp.where(second_valid, row_max, -MASKED)
    return jnp.concatenate(
        [
            jnp.exp2((part - top) * EXPONENT_SCALE).astype(jnp.bfloat16)
            for part, top in ((own, row_max), (first, first_max), (second, second_max))
        ],
        axis=1,
    )


def normalised(mixture):
    return (mixture[:, :HEAD_SIZE] * (1.0 / mixture[:, HEAD_SIZE:])).astype(jnp.bfloat16)


def mix(weights, values):
    return normalised(jnp.dot(weights, values, preferred_element_type=jnp.float32))


def attend_head(queries, keys, values, causal, first_valid, second_valid):
    return mix(weigh(queries, keys, causal, first_valid, second_valid), values)


def with_ones(values):
    return jnp.concatenate([values, jnp.ones_like(values)], axis=1)


def causal_mask(rows):
    return lax.broadcasted_iota(jnp.int32, (rows, rows), 1) <= lax.broadcasted_iota(
        jnp.int32, (rows, rows), 0
    )


def parts_of(rows):
    order = ((0, 0, 2), (1, 0, 2), (0, 1, 2), (1, 1, 2), (0, 2, 2), (0, 3, 2), (1, 2, 4), (1, 3, 4))
    return [
        (kind, g, rows // cuts * i, rows // cuts) for kind, g, cuts in order for i in range(cuts)
    ]


def relay_kernel(rows, selected_hbm, query_hbm, key_hbm, value_hbm, out_ref, *scratch):
    heads = KEY_VALUE_HEADS
    parts = parts_of(rows)
    chunks = len(parts)
    together = [k for k, count in enumerate(GROUPS) for _ in range(count)]
    stores = scratch[:chunks]
    outgoing = scratch[chunks : 2 * chunks]
    gathered = scratch[2 * chunks : 3 * chunks]
    (
        query_ref,
        weight_ref,
        total_ref,
        request_vmem,
        request_smem,
        selected_ref,
        local_sem,
        request_send,
        request_recv,
        layer_recv,
        below_recv,
        deliver_recv,
        pass_send,
        deliver_send,
    ) = scratch[3 * chunks :]
    unit = rows // SIDE
    top = LAYERS - 1
    me = lax.axis_index("ctx")
    layer = me // SIDE
    place = me % SIDE

    def quarter_of(c, q):
        size = parts[c][3] // SIDE
        return pl.ds(q * size, size)

    def on_layer(*layers):
        wanted = layer == layers[0]
        for other in layers[1:]:
            wanted = jnp.logical_or(wanted, layer == other)
        return pl.when(wanted)

    def peer(offset):
        return layer * SIDE + (place + offset) % SIDE

    def remote(src, dst, send, recv, target):
        return pltpu.make_async_remote_copy(
            src_ref=src,
            dst_ref=dst,
            send_sem=send,
            recv_sem=recv,
            device_id={"ctx": target},
            device_id_type=MESH,
        )

    def stacked(pieces):
        return query_ref.at[pl.ds(0, pieces * unit * HEAD_SIZE // query_ref.shape[1]), :]

    def pack(c):
        kind, g, start, count = parts[c]
        return pltpu.make_async_copy(
            (key_hbm, value_hbm)[kind].at[pl.ds(start, count), pl.ds(g * HEAD_SIZE, HEAD_SIZE)],
            gathered[c].at[0],
            local_sem.at[1],
        )

    def fetch_queries(g):
        columns = pl.ds(g * GROUP_WIDTH * HEAD_SIZE, GROUP_WIDTH * HEAD_SIZE)
        return pltpu.make_async_copy(
            query_hbm.at[:, columns], query_ref.at[:, columns], local_sem.at[2]
        )

    def request(offset):
        slot = request_vmem.at[place]
        return remote(
            slot, slot, request_send, request_recv.at[0], peer(offset)
        )

    def request_down(q):
        return remote(
            request_vmem.at[place],
            request_vmem.at[SIDE + place],
            request_send,
            request_recv.at[1],
            (top - 1) * SIDE + q,
        )

    def wait_bytes(ref, semaphore):
        pltpu.make_async_copy(ref, ref, semaphore).wait()

    def spread(c, offset):
        target = (place + offset) % SIDE
        return remote(
            gathered[c].at[0, quarter_of(c, target), :],
            stores[c].at[me],
            pass_send,
            layer_recv.at[together[c]],
            peer(offset),
        )

    def direct(c, turn):
        q = (place // 2 * 2 + 2 + turn) % SIDE
        return remote(
            gathered[c].at[0, quarter_of(c, q), :],
            stores[c].at[me],
            pass_send,
            below_recv.at[c],
            (layer + 1) % LAYERS * SIDE + q,
        )

    def chain(c, source_layer):
        part = stores[c].at[pl.ds(source_layer * SIDE, SIDE)]
        return remote(
            part,
            part,
            pass_send,
            below_recv.at[c],
            (layer + 1) % LAYERS * SIDE + place,
        )

    def deliver(c, offset):
        return remote(
            outgoing[c].at[offset - 1],
            gathered[c].at[pl.ds(1, 2), quarter_of(c, place), :],
            deliver_send,
            deliver_recv.at[together[c]],
            peer(offset),
        )

    def choices_of(q):
        return (1,) if q == SIDE - 1 else (0, 1)

    def deliver_up(c, q):
        span = len(choices_of(q))
        return remote(
            outgoing[c].at[SIDE - 1 + q, pl.ds(2 - span, span)],
            gathered[c].at[pl.ds(3 - span, span), quarter_of(c, place), :],
            pass_send,
            deliver_recv.at[together[c]],
            top * SIDE + q,
        )

    def dense(c, source, target, slot, recv):
        return remote(
            gathered[c].at[source],
            gathered[c].at[3 + slot],
            pass_send,
            recv.at[together[c] if recv is layer_recv else c],
            top * SIDE + target,
        )

    def dense_of(c, q):
        plan = {
            0: ((1, 0, below_recv), (2, 0, layer_recv)),
            1: ((3, 1, layer_recv),),
            2: ((3, 2, below_recv),),
            3: (),
        }[q]
        return [dense(c, 0, *target) for target in plan]

    def relay_of(c, q):
        return dense(c, 3, 3, 0, below_recv) if q == 2 else dense(c, 4, 2, 1, below_recv)

    def on_place(q):
        return pl.when(me == top * SIDE + q)

    fetch_selected = pltpu.make_async_copy(selected_hbm, selected_ref, local_sem.at[0])
    fetch_selected.start()
    for c in range(chunks):
        pack(c).start()
    for g in range(heads):
        fetch_queries(g).start()

    barrier = pltpu.get_barrier_semaphore()
    for offset in range(1, SIDE):
        pl.semaphore_signal(barrier, inc=1, device_id={"ctx": peer(offset)}, device_id_type=MESH)

    @pl.when(layer > 0)
    def _():
        for q in range(SIDE):
            pl.semaphore_signal(
                barrier, inc=1, device_id={"ctx": (layer - 1) * SIDE + q}, device_id_type=MESH
            )

    @pl.when(layer < top)
    def _():
        for q in range(SIDE):
            pl.semaphore_signal(
                barrier, inc=1, device_id={"ctx": (layer + 1) * SIDE + q}, device_id_type=MESH
            )

    neighbour_layers = jnp.minimum(layer, 1) + jnp.minimum(top - layer, 1)
    pl.semaphore_wait(barrier, SIDE - 1 + SIDE * neighbour_layers)

    wait_bytes(stacked(2 * heads * SIDE), local_sem.at[1])

    @on_layer(0, 1)
    def _():
        for c in range(AHEAD):
            for q in range(SIDE):
                direct(c, q).start()

    late = jnp.logical_and(layer == 1, place >= SIDE // 2)

    @pl.when(jnp.logical_or(layer == 0, late))
    def _():
        for q in range(SIDE):
            direct(AHEAD, q).start()

    @on_layer(0)
    def _():
        for c in range(AHEAD + 1, DIRECT):
            for q in range(SIDE):
                direct(c, q).start()

    fetch_selected.wait()
    lane = lax.broadcasted_iota(jnp.int32, (1, 128), 1)
    request_vmem[place] = jnp.where(lane == 0, selected_ref[0, 0], selected_ref[0, 1])

    @on_layer(top)
    def _():
        for q in range(SIDE):
            request_down(q).start()

    @pl.when(layer < top)
    def _():
        for offset in range(1, SIDE):
            request(offset).start()

    for c in range(chunks):
        @pl.when(layer < top)
        def _():
            for offset in range(1, SIDE):
                spread(c, offset).start()
            stores[c][me] = gathered[c][0, quarter_of(c, place), :]

        for q in range(SIDE - 1):

            @on_place(q)
            def _():
                for copy in dense_of(c, q):
                    copy.start()

    first_valid = selected_ref[0, 0] < me
    second_valid = jnp.logical_and(
        selected_ref[0, 1] < me, selected_ref[0, 1] != selected_ref[0, 0]
    )
    causal = causal_mask(rows)

    def slot_of(choice):
        wanted = selected_ref[0, choice]
        local = jnp.logical_and(layer == top, wanted >= top * SIDE)
        return jnp.where(local, 3 + wanted - top * SIDE, 1 + choice)

    def rows_from(c, slot):
        return gathered[c][slot_of(slot - 1) if slot else 0]

    def wait_pieces(c, pieces, semaphore):
        wait_bytes(stores[c].at[pl.ds(0, pieces)], semaphore.at[c])

    def wait_group(c, pieces, semaphore):
        k = together[c]
        if c == sum(GROUPS[:k]):
            size = GROUPS[k] * pieces * parts[c][3] // SIDE * 2 * HEAD_SIZE
            wait_bytes(total_ref.at[0, pl.ds(0, size // (8 * HEAD_SIZE))], semaphore.at[k])

    @on_layer(1)
    def _():
        for c in range(AHEAD):
            wait_pieces(c, SIDE, below_recv)
            chain(c, 0).start()

        @pl.when(place < SIDE // 2)
        def _():
            for q in range(SIDE):
                direct(AHEAD, q).start()

        for c in range(AHEAD + 1, DIRECT):
            for q in range(SIDE):
                direct(c, q).start()

    @pl.when(layer < top)
    def _():
        wait_bytes(request_vmem.at[pl.ds(0, SIDE - 1)], request_recv.at[0])

    @on_layer(top - 1)
    def _():
        wait_bytes(request_vmem.at[pl.ds(0, SIDE)], request_recv.at[1])

    @pl.when(layer != top - 1)
    def _():
        for q in range(SIDE):
            request_vmem[SIDE + q] = jnp.zeros((1, 128), jnp.int32)

    @on_layer(top)
    def _():
        for offset in range(1, SIDE):
            request_vmem[(place + offset) % SIDE] = jnp.zeros((1, 128), jnp.int32)

    to_smem = pltpu.make_async_copy(request_vmem, request_smem, local_sem.at[0])
    to_smem.start()
    to_smem.wait()

    def hand_out(c):
        for offset in range(1, SIDE):
            for choice in range(2):
                wanted = request_smem[(place + offset) % SIDE, 0, choice]
                outgoing[c][offset - 1, choice] = stores[c][wanted]
            deliver(c, offset).start()
        for choice in range(2):
            gathered[c][1 + choice, quarter_of(c, place), :] = stores[c][request_smem[place, 0, choice]]

    def hand_up(c):
        for q in range(SIDE):
            for choice in choices_of(q):
                wanted = jnp.minimum(request_smem[SIDE + q, 0, choice], top * SIDE - 1)
                outgoing[c][SIDE - 1 + q, choice] = stores[c][wanted]
            deliver_up(c, q).start()

    def serve_bottom(c):
        wait_group(c, SIDE - 1, layer_recv)
        if c >= DIRECT:
            chain(c, 0).start()
        hand_out(c)

    def serve_second(c):
        if c >= AHEAD:
            wait_pieces(c, SIDE, below_recv)
            chain(c, 0).start()
        if c == 0:
            for early in range(DIRECT):
                wait_group(early, SIDE - 1, layer_recv)
        if DIRECT <= c + 1 < chunks:
            wait_group(c + 1, SIDE - 1, layer_recv)
            chain(c + 1, 1).start()
        hand_out(c)

    def serve_third(c):
        wait_group(c, SIDE - 1, layer_recv)
        wait_pieces(c, 2 * SIDE, below_recv)
        hand_up(c)
        hand_out(c)

    def serve_top(c):
        @pl.when(place >= 2)
        def _():
            wait_group(c, SIDE, layer_recv)

        for q in (2, 3):

            @on_place(q)
            def _():
                relay_of(c, q).start()

    def serve(step):
        works = (serve_bottom, serve_second, serve_third, serve_top)
        for number, (work, plan) in enumerate(zip(works, SERVED)):
            if plan[step] < plan[step + 1]:

                @on_layer(number)
                def _():
                    for c in range(plan[step], plan[step + 1]):
                        work(c)

    def wait_delivery(c):
        @pl.when(layer < top)
        def _():
            wait_group(c, 2 * (SIDE - 1), deliver_recv)

        for q in range(SIDE):

            @on_place(q)
            def _():
                wait_group(c, SIDE * len(choices_of(q)), deliver_recv)
                if q > 0:
                    wait_pieces(c, SIDE * (2 if q == 3 else 1), below_recv)

    def head_columns(g, index):
        return pl.ds((g * GROUP_WIDTH + index) * HEAD_SIZE, HEAD_SIZE)

    def weigh_group(run, heads_of=range(GROUP_WIDTH)):
        if heads_of[0] == 0:
            for c in run:
                wait_delivery(c)
        g = parts[run[0]][1]
        keys = jnp.concatenate([rows_from(c, slot) for slot in range(3) for c in run], axis=0)
        for index in heads_of:
            weight_ref[g % 2 * GROUP_WIDTH + index] = weigh(
                query_ref[:, head_columns(g, index)], keys, causal, first_valid, second_valid
            )

    def mix_group(arriving, runs, begins=True, ends=True):
        for c in arriving:
            wait_delivery(c)
        g = parts[arriving[0]][1]
        values = with_ones(
            jnp.concatenate([rows_from(c, slot) for slot, run in runs for c in run], axis=0)
        )
        for index in range(GROUP_WIDTH):
            weights = jnp.concatenate(
                [
                    weight_ref[
                        g % 2 * GROUP_WIDTH + index,
                        :,
                        pl.ds(slot * rows + parts[run[0]][2], sum(parts[c][3] for c in run)),
                    ]
                    for slot, run in runs
                ],
                axis=1,
            )
            mixture = jnp.dot(weights, values, preferred_element_type=jnp.float32)
            if not begins:
                mixture += total_ref[index]
            if ends:
                out_ref[:, head_columns(g, index)] = normalised(mixture)
            else:
                total_ref[index] = mixture

    def mix_whole(*run):
        mix_group(run, [(slot, run) for slot in range(3)])

    low, high = range(GROUP_WIDTH // 2), range(GROUP_WIDTH // 2, GROUP_WIDTH)
    serve(0)
    wait_bytes(query_ref, local_sem.at[2])
    weigh_group((0, 1))
    serve(1)
    mix_whole(2, 3)
    serve(2)
    weigh_group((4, 5))
    serve(3)
    mix_whole(6, 7)
    serve(4)
    weigh_group((8, 9), low)
    serve(5)
    weigh_group((8, 9), high)
    serve(6)
    weigh_group((10, 11), low)
    serve(7)
    weigh_group((10, 11), high)
    serve(8)
    mix_whole(12, 13, 14, 15)
    mix_group((16, 17), [(0, (16, 17, 18, 19)), (1, (16, 17)), (2, (16, 17))], ends=False)
    mix_group((18, 19), [(1, (18, 19)), (2, (18, 19))], begins=False)

    full = 2 * heads
    within = full * (SIDE - 1)
    passed = (
        within + full * SIDE,
        within + full * SIDE + full * SIDE,
        within + full * (2 * SIDE - 1),
    )
    for number, pieces in enumerate(passed):

        @on_layer(number)
        def _():
            wait_bytes(stacked(pieces), pass_send)
            wait_bytes(weight_ref.at[pl.ds(0, 2)], deliver_send)
            wait_bytes(request_vmem.at[pl.ds(0, SIDE - 1)], request_send)

    @on_layer(top)
    def _():
        wait_bytes(request_vmem.at[pl.ds(0, SIDE)], request_send)

    for q, blocks in enumerate((2, 1, 2, 1)):

        @on_place(q)
        def _():
            wait_bytes(stacked(full * blocks * SIDE), pass_send)


def relayed(queries, all_key_states, all_value_states, selected):
    rows = queries.shape[0]
    counts = [count for _, _, _, count in parts_of(rows)]
    chunks = len(counts)
    blocks = LAYERS * SIDE
    kind = all_key_states.dtype
    dma = pltpu.SemaphoreType.DMA
    return pl.pallas_call(
        functools.partial(relay_kernel, rows),
        out_shape=pltpu.VMEM(queries.shape, queries.dtype),
        in_specs=[pl.BlockSpec(memory_space=pltpu.HBM)] * 4,
        out_specs=pl.BlockSpec(memory_space=pltpu.VMEM),
        scratch_shapes=[pltpu.VMEM((blocks, n // SIDE, HEAD_SIZE), kind) for n in counts]
        + [pltpu.VMEM((2 * SIDE - 1, 2, n // SIDE, HEAD_SIZE), kind) for n in counts]
        + [pltpu.VMEM((6, n, HEAD_SIZE), kind) for n in counts]
        + [
            pltpu.VMEM(queries.shape, queries.dtype),
            pltpu.VMEM((2 * GROUP_WIDTH, rows, 3 * rows), kind),
            pltpu.VMEM((GROUP_WIDTH, rows, 2 * HEAD_SIZE), jnp.float32),
            pltpu.VMEM((2 * SIDE, 1, 128), jnp.int32),
            pltpu.SMEM((2 * SIDE, 1, 128), jnp.int32),
            pltpu.SMEM((1, 2), jnp.int32),
            dma((3,)),
            dma,
            dma((2,)),
            dma((len(GROUPS),)),
            dma((chunks,)),
            dma((len(GROUPS),)),
            dma,
            dma,
        ],
        compiler_params=pltpu.CompilerParams(
            collective_id=0, has_side_effects=True, vmem_limit_bytes=123 * 2**19
        ),
    )(selected, queries, all_key_states, all_value_states)


def attend_kernel(valid_ref, query_ref, key_ref, value_ref, out_ref):
    rows = query_ref.shape[0]
    causal = lax.broadcasted_iota(jnp.int32, (rows, rows), 1) <= lax.broadcasted_iota(
        jnp.int32, (rows, rows), 0
    )
    out_ref[...] = attend_head(
        query_ref[...],
        key_ref[...],
        with_ones(value_ref[...]),
        causal,
        valid_ref[0] != 0,
        valid_ref[1] != 0,
    )


def exchanged(queries, all_key_states, all_value_states, selected):
    devices = lax.axis_size("ctx")
    me = lax.axis_index("ctx")
    rows, width = all_key_states.shape
    exchange = functools.partial(
        lax.all_to_all, axis_name="ctx", split_axis=0, concat_axis=0, tiled=True
    )
    both = jnp.concatenate([all_key_states, all_value_states], axis=1)
    requests = lax.all_gather(selected, "ctx", axis=0, tiled=True)
    held = exchange(both.reshape(devices, rows // devices, 2 * width))
    flat = held.reshape(devices, rows // devices * 2 * width)
    numbers = jnp.arange(devices, dtype=requests.dtype)

    def picked(choice):
        pick = (requests[:, choice, None] == numbers[None, :]).astype(flat.dtype)
        taken = jnp.dot(pick, flat, preferred_element_type=jnp.float32).astype(flat.dtype)
        return exchange(taken.reshape(held.shape)).reshape(rows, 2 * width)

    chosen = [picked(choice) for choice in range(2)]
    everything = jnp.concatenate([both] + chosen, axis=0)
    first, second = selected[0, 0], selected[0, 1]
    valid = jnp.stack([first < me, jnp.logical_and(second < me, second != first)])
    return pl.pallas_call(
        attend_kernel,
        out_shape=jax.ShapeDtypeStruct(queries.shape, queries.dtype),
        grid=(QUERY_HEADS,),
        in_specs=[
            pl.BlockSpec(memory_space=pltpu.SMEM),
            pl.BlockSpec((rows, HEAD_SIZE), lambda h: (0, h)),
            pl.BlockSpec((3 * rows, HEAD_SIZE), lambda h: (0, h // GROUP_WIDTH)),
            pl.BlockSpec((3 * rows, HEAD_SIZE), lambda h: (0, KEY_VALUE_HEADS + h // GROUP_WIDTH)),
        ],
        out_specs=pl.BlockSpec((rows, HEAD_SIZE), lambda h: (0, h)),
    )(valid.astype(jnp.int32), queries, everything, everything)


def solution(mesh):
    placed = P(("groups", "ctx"), None)
    local = relayed if mesh.shape["ctx"] == LAYERS * SIDE else exchanged
    return jax.shard_map(
        local, mesh=mesh, in_specs=(placed,) * 4, out_specs=placed, check_vma=False
    )
```
